256 devices in a mesh: tm: 8 (over x, core), rows: 32 (over z, y).
Axes of the slice: x: 4, y: 4, z: 8, core: 2. Of those that a mesh axis runs over, the one named last changes fastest.
Arguments:
- features: bfloat16 [2, 32, 48, 256, 128], P(None, 'tm', None, 'rows'), may hold values from -6 to 6
- out_grad: bfloat16 [2, 32, 48, 256, 128], P(None, 'tm', None, 'rows'), may hold values from -36 to 36
- decay_rate: float32 [2, 32, 48], replicated, may hold values from 0.14 to 0.995
- clip_start: int32 [2], replicated, may hold values from 1 to 31
- conv_kernel: bfloat16 [9, 48, 48], replicated, may hold values from -0.3125 to 0.3125
- context_mix: bfloat16 [48, 64], replicated, may hold values from -0.875 to 0.875
- feature_mix: bfloat16 [48, 64], replicated, may hold values from -0.875 to 0.875
- output_mix: bfloat16 [64, 48], replicated, may hold values from -0.75 to 0.75
Outputs:
- recon: bfloat16 [2, 32, 48, 256, 128], P(None, 'tm', None, 'rows')
- grad_decay: float32 [2, 32, 48], P(None, 'tm')
- grad_conv: float32 [9, 48, 48], replicated
- grad_context_mix: float32 [48, 64], replicated
- grad_feature_mix: float32 [48, 64], replicated
- grad_output_mix: float32 [64, 48], replicated
The draws below stay inside these ranges and needn't reach their ends.
All inputs are finite; a program needn't handle non-finite values.
Results may differ from the reference program's by a relative error of at most 0.0075.
Values may be sent and summed in bfloat16 or wider, within the bound.
No kernel may reach another device: no remote copies, remote signals or barrier semaphores. Data moves between devices by JAX's collectives and lax.ppermute only.
A program may use at most 64 MiB of HBM per device.

```python
import math
import jax
import jax.numpy as jnp
from jax import lax

CTX = 48
HID = 64
CLIP_NUMBER = 2
COLS = 128
PICTURE_COUNT = 32
HEIGHT = 256


def draw_out_grad(key, part):
    first_key = jax.random.fold_in(key, 0)
    shape = (CLIP_NUMBER, PICTURE_COUNT, CTX, HEIGHT, COLS)
    frame_pos = jnp.arange(PICTURE_COUNT, dtype=jnp.float32) / max(PICTURE_COUNT - 1, 1)
    row_pos = jnp.arange(HEIGHT, dtype=jnp.float32) / max(HEIGHT - 1, 1)
    scaling = jnp.exp(jnp.log(3.0) * frame_pos)[:, None, None, None] * jnp.exp(jnp.log(3.0) * row_pos)[None, None, :, None]
    nominal_level = jnp.clip(jax.random.normal(first_key, shape, jnp.float32), -4.0, 4.0)
    return (nominal_level * scaling[None]).astype(jnp.bfloat16)


def draw_decay_rate(key, part):
    stochastic_seeds = jax.random.split(key, 6)
    slow_share = 0.5
    slow_mask = jax.random.uniform(stochastic_seeds[0], (CLIP_NUMBER, 1, CTX), jnp.float32) < slow_share
    slow_rate = 1.0 - jnp.exp(jax.random.uniform(stochastic_seeds[1], (CLIP_NUMBER, 1, CTX), jnp.float32, jnp.log(0.005), jnp.log(0.06)))
    fast_rate = jax.random.uniform(stochastic_seeds[2], (CLIP_NUMBER, 1, CTX), jnp.float32, 0.3, 0.7)
    nominal_level = jnp.where(slow_mask, slow_rate, fast_rate)
    small_perturbation = jax.random.uniform(stochastic_seeds[3], (CLIP_NUMBER, PICTURE_COUNT, CTX), jnp.float32, 0.97, 1.0)
    surge_peak = jax.random.uniform(stochastic_seeds[4], (CLIP_NUMBER, PICTURE_COUNT, 1), jnp.float32) < 0.12
    surge_factor = jax.random.uniform(stochastic_seeds[5], (CLIP_NUMBER, PICTURE_COUNT, 1), jnp.float32, 0.5, 0.8)
    return (nominal_level * small_perturbation * jnp.where(surge_peak, surge_factor, 1.0)).astype(jnp.float32)


def levels(rng, extent, cuts, smallest, largest):
    def one(axis_at, shards_of):
        heights = jax.random.uniform(jax.random.fold_in(jax.random.fold_in(rng, 6), axis_at), (shards_of,), jnp.float32, smallest / len(cuts), largest / len(cuts))
        return jnp.repeat(jnp.exp(heights), extent[axis_at] // shards_of).reshape((-1,) + (1,) * (len(extent) - axis_at - 1))

    level = one(*cuts[0])
    for cut in cuts[1:]:
        level = level * one(*cut)
    return level


def noise(key, shape, deviation, bound, cuts=(), kind=jnp.bfloat16):
    loudness = levels(key, shape, cuts, -0.22, 0.18) if cuts else 1.0
    values = jax.random.normal(key, shape, jnp.float32) * deviation * loudness
    return jnp.minimum(jnp.maximum(values, -bound), bound).astype(kind)


def setup_inputs(seed: int = 0) -> dict:
    keys = jax.random.split(jax.random.key(seed), 9)
    features = noise(keys[0], (CLIP_NUMBER, PICTURE_COUNT, CTX, HEIGHT, COLS), 1.0, 6.0, ((1, 8), (3, 32)))
    out_grad = draw_out_grad(jax.random.fold_in(keys[8], 71), 0)
    decay_rate = draw_decay_rate(jax.random.fold_in(keys[8], 71), 0)
    clip_start = jax.random.randint(keys[3], (CLIP_NUMBER,), 1, PICTURE_COUNT).astype(jnp.int32)
    conv_kernel = noise(keys[4], (9, CTX, CTX), (9 * CTX) ** -0.5, 0.3125)
    context_mix = noise(keys[5], (CTX, HID), CTX ** -0.5, 0.875)
    feature_mix = noise(keys[6], (CTX, HID), CTX ** -0.5, 0.875)
    output_mix = noise(keys[7], (HID, CTX), HID ** -0.5, 0.75)
    return dict(features=features, out_grad=out_grad, decay_rate=decay_rate, clip_start=clip_start, conv_kernel=conv_kernel, context_mix=context_mix, feature_mix=feature_mix, output_mix=output_mix)


def conv_frame(frame, conv_kernel):
    padded = jnp.pad(frame, ((0, 0), (1, 1), (1, 1)))
    summed = jnp.zeros((CTX, HEIGHT, COLS), jnp.float32)
    for position in range(9):
        shifted = padded[:, position // 3:position // 3 + HEIGHT, position % 3:position % 3 + COLS]
        summed = summed + jnp.einsum('chw,cd->dhw', shifted.astype(jnp.float32), conv_kernel[position].astype(jnp.float32))
    return summed

def one_sequence(features, out_grad, decay_rate, clip_start, conv_kernel, context_mix, feature_mix, output_mix):
    frame_ids = jnp.arange(PICTURE_COUNT, dtype=jnp.int32)
    keep = (frame_ids != clip_start).astype(jnp.float32)
    zero_state = jnp.zeros((CTX, HEIGHT, COLS), jnp.float32)

    def forward(state, inputs):
        frame, gamma, keep_now = inputs
        update = conv_frame(frame, conv_kernel).astype(jnp.bfloat16)
        prior = keep_now * state
        state = gamma[:, None, None] * prior + update.astype(jnp.float32)
        return (state, prior)
    unused, priors = lax.scan(forward, zero_state, (features, decay_rate, keep))

    def backward(carry, inputs):
        state, kernel_grad, ctx_mix_grad, feat_mix_grad, out_mix_grad = carry
        frame, grad_frame, prior, gamma, keep_now = inputs
        prior_low = prior.astype(jnp.bfloat16)
        preact = jnp.einsum('chw,ck->khw', prior_low.astype(jnp.float32), context_mix.astype(jnp.float32))
        preact = preact + jnp.einsum('chw,ck->khw', frame.astype(jnp.float32), feature_mix.astype(jnp.float32))
        hidden = jax.nn.silu(preact).astype(jnp.bfloat16)
        recon = jnp.einsum('khw,kc->chw', hidden.astype(jnp.float32), output_mix.astype(jnp.float32)).astype(jnp.bfloat16)
        hidden_grad = jnp.einsum('chw,kc->khw', grad_frame.astype(jnp.float32), output_mix.astype(jnp.float32))
        gate_value = jax.nn.sigmoid(preact)
        pre_grad = (hidden_grad * gate_value * (1.0 + preact * (1.0 - gate_value))).astype(jnp.bfloat16)
        out_mix_grad = out_mix_grad + jnp.einsum('khw,chw->kc', hidden.astype(jnp.float32), grad_frame.astype(jnp.float32))
        ctx_mix_grad = ctx_mix_grad + jnp.einsum('chw,khw->ck', prior_low.astype(jnp.float32), pre_grad.astype(jnp.float32))
        feat_mix_grad = feat_mix_grad + jnp.einsum('chw,khw->ck', frame.astype(jnp.float32), pre_grad.astype(jnp.float32))
        prior_grad = jnp.einsum('khw,ck->chw', pre_grad.astype(jnp.float32), context_mix.astype(jnp.float32))
        gamma_grad = lax.optimization_barrier(jnp.sum(prior * state, axis=(1, 2)))
        update_grad = state.astype(jnp.bfloat16)
        padded = jnp.pad(frame, ((0, 0), (1, 1), (1, 1)))
        products = []
        for position in range(9):
            shifted = padded[:, position // 3:position // 3 + HEIGHT, position % 3:position % 3 + COLS]
            products.append(jnp.einsum('chw,dhw->cd', shifted.astype(jnp.float32), update_grad.astype(jnp.float32)))
        kernel_grad = kernel_grad + jnp.stack(products, 0)
        new_state = keep_now * (gamma[:, None, None] * state + prior_grad)
        return ((new_state, kernel_grad, ctx_mix_grad, feat_mix_grad, out_mix_grad), (recon, gamma_grad))
    start = (zero_state, jnp.zeros((9, CTX, CTX), jnp.float32), jnp.zeros((CTX, HID), jnp.float32), jnp.zeros((CTX, HID), jnp.float32), jnp.zeros((HID, CTX), jnp.float32))
    final, outputs = lax.scan(backward, start, (features, out_grad, priors, decay_rate, keep), reverse=True)
    return (outputs[0], outputs[1], final[1], final[2], final[3], final[4])

def reference(features, out_grad, decay_rate, clip_start, conv_kernel, context_mix, feature_mix, output_mix):

    def per_sequence(inputs):
        return one_sequence(inputs[0], inputs[1], inputs[2], inputs[3], conv_kernel, context_mix, feature_mix, output_mix)
    results = lax.map(per_sequence, (features, out_grad, decay_rate, clip_start))
    scale_all = 1.0 / math.sqrt(CLIP_NUMBER * PICTURE_COUNT * HEIGHT * COLS)
    scale_pix = 1.0 / math.sqrt(HEIGHT * COLS)
    recon = results[0]
    grad_decay = results[1] * scale_pix
    grad_conv = lax.optimization_barrier(jnp.sum(results[2], axis=0)) * scale_all
    grad_context_mix = lax.optimization_barrier(jnp.sum(results[3], axis=0)) * scale_all
    grad_feature_mix = lax.optimization_barrier(jnp.sum(results[4], axis=0)) * scale_all
    grad_output_mix = lax.optimization_barrier(jnp.sum(results[5], axis=0)) * scale_all
    return (recon, grad_decay, grad_conv, grad_context_mix, grad_feature_mix, grad_output_mix)
```

```python
import math

import jax
import jax.numpy as jnp
from jax import lax
from jax.experimental import pallas as pl
from jax.experimental.pallas import tpu as pltpu
from jax.sharding import PartitionSpec as P

F32 = jnp.float32
BF16 = jnp.bfloat16
LANES = 128
CORES, XS, YS, ZS = 2, 4, 4, 8

CORE_SWAP = [(i, i ^ 1) for i in range(CORES * XS)]


def x_shift(step):
    count = CORES * XS
    return [(i, (i + CORES * step) % count) for i in range(count)]


def y_shift(step):
    return [(i, i // YS * YS + (i + step) % YS) for i in range(YS * ZS)]


Z_GROUPS = [[z * YS + y for z in range(ZS)] for y in range(YS)]


def mm(a, b):
    return jnp.dot(a, b, preferred_element_type=F32)


def mm_nt(a, b):
    return lax.dot_general(a, b, (((1,), (1,)), ((), ())), preferred_element_type=F32)


def shifted(value, step):
    lane = lax.broadcasted_iota(jnp.int32, (value.shape[0], LANES), 1)
    inside = lane < LANES - 1 if step > 0 else lane > 0
    blocks = []
    for at in range(0, value.shape[1], LANES):
        rolled = pltpu.roll(value[:, at : at + LANES], (-step) % LANES, 1)
        blocks.append(jnp.where(inside, rolled, 0.0))
    return jnp.concatenate(blocks, 1)


def wide(value, width):
    return jnp.concatenate([value] * (width // LANES), 1)


def row_taps(low, x, high):
    padded = jnp.concatenate([low, x, high], 1)
    width = x.shape[1]
    return jnp.concatenate([padded[:, LANES * a : LANES * a + width] for a in range(3)], 0)


def conv_kernel_body(keep_ref, x_ref, low_ref, high_ref, w_ref, gamma_ref, upd_ref, end_ref):
    seq = pl.program_id(0)
    frames, channels, width = x_ref.shape
    state = jnp.zeros((channels, width), F32)
    for f in range(frames):
        taps = row_taps(low_ref[f], x_ref[f], high_ref[f])
        y = mm(w_ref[...], taps)
        out = (
            y[channels : 2 * channels]
            + shifted(y[:channels], -1)
            + shifted(y[2 * channels :], 1)
        ).astype(BF16)
        upd_ref[f] = out
        decay = gamma_ref[f] * keep_ref[seq * frames + f]
        state = wide(decay, width) * state + out.astype(F32)
    end_ref[0] = state.astype(BF16)


def join_body(
    keep_ref, upd_ref, x_ref, og_ref, entry_ref, gamma_ref, mix_ref, out_ref, out_t_ref, ctx_ref,
    recon_ref, prior_ref, pgrad_ref, end_ref, mixg_ref,
):
    seq = pl.program_id(0)
    frames, channels, width = x_ref.shape
    hidden_count = mix_ref.shape[0]

    @pl.when(seq == 0)
    def _():
        mixg_ref[...] = jnp.zeros_like(mixg_ref)

    state = entry_ref[0]
    for f in range(frames):
        prior = state * keep_ref[seq * frames + f]
        prior_ref[f] = prior
        state = wide(gamma_ref[f], width) * prior + upd_ref[f].astype(F32)
    total = jnp.zeros(mixg_ref.shape, F32)
    fill = jnp.zeros((LANES - hidden_count - channels, width), BF16)
    back = jnp.zeros((channels, width), F32)
    for f in reversed(range(frames)):
        joined = jnp.concatenate([prior_ref[f].astype(BF16), x_ref[f]], 0)
        preact = mm(mix_ref[...], joined)
        gate = 1.0 / (1.0 + jnp.exp(-preact))
        hidden = (preact * gate).astype(BF16)
        og = og_ref[f]
        recon_ref[f] = mm(out_t_ref[...], hidden).astype(BF16)
        hidden_grad = mm(out_ref[...], og)
        pre_grad = (hidden_grad * gate * (1.0 + preact * (1.0 - gate))).astype(BF16)
        prior_grad = mm(ctx_ref[...], pre_grad)
        pgrad_ref[f] = prior_grad
        back = (wide(gamma_ref[f], width) * back + prior_grad) * keep_ref[seq * frames + f]
        total = total + mm_nt(
            jnp.concatenate([joined, hidden], 0), jnp.concatenate([pre_grad, og, fill], 0)
        )
    end_ref[0] = back.astype(BF16)
    mixg_ref[...] += total


def grad_body(
    keep_ref, tm_ref, x_ref, low_ref, high_ref, prior_ref, pgrad_ref, entry_ref, gamma_ref, mixg_ref,
    pack_ref,
):
    seq = pl.program_id(0)
    frames, channels, width = x_ref.shape
    hidden_count = mixg_ref.shape[0] - 2 * channels

    @pl.when(seq == 0)
    def _():
        lane = lax.broadcasted_iota(jnp.int32, (2 * channels, LANES), 1)
        mixg = jnp.where(lane < hidden_count, mixg_ref[: 2 * channels], 0.0)
        lane = lane[:hidden_count]
        outg = jnp.where(
            (lane >= hidden_count) & (lane < hidden_count + channels), mixg_ref[2 * channels :], 0.0
        )
        pack_ref[0] = jnp.zeros_like(pack_ref[0])
        pack_ref[1, :hidden_count] = mixg[:hidden_count] + outg
        pack_ref[1, hidden_count : 2 * channels] = mixg[hidden_count:]
        pack_ref[1, 2 * channels :] = jnp.zeros((channels, LANES), F32)

    lane = lax.broadcasted_iota(jnp.int32, (channels, LANES), 1)
    state = entry_ref[0]
    first = jnp.zeros((3 * channels, LANES), F32)
    second = jnp.zeros((3 * channels, LANES), F32)
    decay_grad = jnp.zeros((channels, LANES), F32)
    rest = 3 * channels - LANES
    blank = jnp.zeros((LANES - rest, width), BF16)
    for f in reversed(range(frames)):
        product = prior_ref[f] * state
        folded = product[:, :LANES]
        for at in range(LANES, width, LANES):
            folded = folded + product[:, at : at + LANES]
        column = jnp.sum(folded, axis=1, keepdims=True)
        slot = (tm_ref[0] * 2 + seq) * frames + f
        decay_grad = decay_grad + jnp.where(lane == slot, column, 0.0)
        u = jnp.concatenate(
            [shifted(state, 1).astype(BF16), state.astype(BF16), shifted(state, -1).astype(BF16)], 0
        )
        taps = row_taps(low_ref[f], x_ref[f], high_ref[f])
        first = first + mm_nt(taps, u[:LANES])
        second = second + mm_nt(taps, jnp.concatenate([blank, u[LANES:]], 0))
        state = (wide(gamma_ref[f], width) * state + pgrad_ref[f]) * keep_ref[seq * frames + f]
    pack_ref[0] += first
    pack_ref[1] += second
    pack_ref[1, 2 * channels :] += decay_grad


def smem():
    return pl.BlockSpec(memory_space=pltpu.SMEM)


def by_seq(shape):
    return pl.BlockSpec(shape, lambda s: (s,) + (0,) * (len(shape) - 1))


def whole(shape):
    return pl.BlockSpec(shape, lambda s: (0,) * len(shape))


PARAMS = pltpu.CompilerParams(vmem_limit_bytes=48 * 1024 * 1024)


def exchange(ends, factors, reverse):
    core = lax.axis_index("tm") % CORES
    chip = lax.axis_index("tm") // CORES
    second = core == 1
    mine = jnp.where(second, ends[1], ends[0])
    other = jnp.where(second, ends[0], ends[1])
    got = lax.ppermute(other, "tm", CORE_SWAP)
    factor = jnp.where(second, factors[1], factors[0]).reshape(XS, CORES, -1)
    here = lax.dynamic_index_in_dim(factor, chip, 0, keepdims=False)
    mine_first = second if reverse else jnp.logical_not(second)
    early = jnp.where(mine_first, mine, got).astype(F32)
    late = jnp.where(mine_first, got, mine).astype(F32)
    early_factor, late_factor = (here[1], here[0]) if reverse else (here[0], here[1])
    chip_end = (late_factor[:, None] * early + late).astype(BF16)
    chip_factor = factor[:, 0] * factor[:, 1]
    entry = None
    weight = jnp.ones_like(chip_factor[0])
    for step in range(1, XS):
        came = lax.ppermute(chip_end, "tm", x_shift(-step if reverse else step)).astype(F32)
        source = chip + step if reverse else chip - step
        there = source < XS if reverse else source >= 0
        term = jnp.where(there, weight, 0.0)[:, None] * came
        entry = term if entry is None else entry + term
        weight = weight * lax.dynamic_index_in_dim(chip_factor, source % XS, 0, keepdims=False)
    to_late = early_factor[:, None] * entry + early
    mine = jnp.where(mine_first, entry, to_late)
    other = jnp.where(mine_first, to_late, entry).astype(BF16)
    got = lax.ppermute(other, "tm", CORE_SWAP).astype(F32)
    return jnp.stack([jnp.where(second, got, mine), jnp.where(second, mine, got)], 0)


def all_sum(pack):
    second = lax.axis_index("tm") % CORES == 1
    mine = jnp.where(second, pack[1], pack[0])
    other = jnp.where(second, pack[0], pack[1]).astype(BF16)
    total = mine + lax.ppermute(other, "tm", CORE_SWAP).astype(F32)
    for axis, shift in (("tm", x_shift), ("rows", y_shift)):
        sent = total.astype(BF16)
        came = [lax.ppermute(sent, axis, shift(step)).astype(F32) for step in (1, 2, 3)]
        total = (sent.astype(F32) + came[1]) + (came[0] + came[2])
    sent = jnp.broadcast_to(total.astype(BF16)[None], (ZS,) + total.shape)
    came = lax.all_to_all(sent, "rows", 0, 0, axis_index_groups=Z_GROUPS)
    mine = jnp.sum(came.astype(F32), axis=0)
    got = lax.ppermute(mine, "tm", CORE_SWAP)
    return jnp.where(second, got, mine), jnp.where(second, mine, got)


def shards(
    features, out_grad, decay_rate, clip_start, conv_kernel, context_mix, feature_mix, output_mix
):
    seqs, frames, channels, rows, cols = features.shape
    hidden_count = context_mix.shape[1]
    tm_count = lax.axis_size("tm")
    rows_count = lax.axis_size("rows")
    all_frames = frames * tm_count
    height = rows * rows_count
    pixels = rows * cols
    scale_all = 1.0 / math.sqrt(seqs * all_frames * height * cols)
    scale_pix = 1.0 / math.sqrt(height * cols)
    tm = lax.axis_index("tm")

    down = [(i, i + 1) for i in range(rows_count - 1)]
    up = [(i + 1, i) for i in range(rows_count - 1)]
    low = lax.ppermute(features[:, :, :, rows - 1].reshape(-1, channels, cols), "rows", down)
    high = lax.ppermute(features[:, :, :, 0].reshape(-1, channels, cols), "rows", up)

    x = features.reshape(seqs * frames, channels, pixels)
    og = out_grad.reshape(seqs * frames, channels, pixels)
    frame_ids = jnp.arange(all_frames, dtype=jnp.int32)
    keep_all = (frame_ids[None, :] != clip_start[:, None]).astype(F32)
    kept = (keep_all[:, :, None] * decay_rate).reshape(seqs, tm_count, frames, channels)
    factors = kept[:, :, 0]
    for f in range(1, frames):
        factors = factors * kept[:, :, f]
    keep = lax.dynamic_slice_in_dim(keep_all, tm * frames, frames, 1).reshape(-1)
    gamma = lax.dynamic_slice_in_dim(decay_rate, tm * frames, frames, 1)
    gamma = jnp.broadcast_to(
        gamma.reshape(seqs * frames, channels, 1), (seqs * frames, channels, LANES)
    )
    taps_w = conv_kernel.reshape(3, 3, channels, channels).transpose(1, 3, 0, 2)
    taps_w = taps_w.reshape(3 * channels, 3 * channels)
    mix = jnp.concatenate([context_mix, feature_mix], 0).T

    xs = by_seq((frames, channels, pixels))
    edge = by_seq((frames, channels, cols))
    one = by_seq((1, channels, pixels))
    gs = by_seq((frames, channels, LANES))
    sds = jax.ShapeDtypeStruct
    full = (seqs * frames, channels, pixels)

    update, ends = pl.pallas_call(
        conv_kernel_body,
        grid=(seqs,),
        in_specs=[smem(), xs, edge, edge, whole(taps_w.shape), gs],
        out_specs=[xs, one],
        out_shape=[sds(full, BF16), sds((seqs, channels, pixels), BF16)],
        compiler_params=PARAMS,
        name="conv",
    )(keep, x, low, high, taps_w, gamma)

    entry = exchange(ends, factors, False)

    mixg_shape = (2 * channels + hidden_count, LANES)
    recon, priors, prior_grads, ends_back, mixg = pl.pallas_call(
        join_body,
        grid=(seqs,),
        in_specs=[
            smem(), xs, xs, xs, one, gs,
            whole(mix.shape), whole(output_mix.shape), whole(output_mix.T.shape),
            whole(context_mix.shape),
        ],
        out_specs=[xs, xs, xs, one, whole(mixg_shape)],
        out_shape=[
            sds(full, BF16), sds(full, F32), sds(full, F32),
            sds((seqs, channels, pixels), BF16), sds(mixg_shape, F32),
        ],
        compiler_params=PARAMS,
        name="join",
    )(keep, update, x, og, entry, gamma, mix, output_mix, output_mix.T, context_mix)

    entry_back = exchange(ends_back, factors, True)

    pack_shape = (2, 3 * channels, LANES)
    pack = pl.pallas_call(
        grad_body,
        grid=(seqs,),
        in_specs=[smem(), smem(), xs, edge, edge, xs, xs, one, gs, whole(mixg_shape)],
        out_specs=whole(pack_shape),
        out_shape=sds(pack_shape, F32),
        compiler_params=PARAMS,
        name="grad",
    )(keep, tm.reshape(1), x, low, high, priors, prior_grads, entry_back, gamma, mixg)

    first, second = all_sum(pack)
    rest = 3 * channels - LANES
    taps_grad = jnp.concatenate([first, second[:, LANES - rest :]], 1)
    taps_grad = taps_grad.reshape(3, channels, 3, channels).transpose(0, 2, 1, 3)
    slots = lax.dynamic_slice_in_dim(
        second[2 * channels :], tm * (seqs * frames), seqs * frames, 1
    )
    return (
        recon.reshape(features.shape),
        slots.T.reshape(seqs, frames, channels) * scale_pix,
        taps_grad.reshape(9, channels, channels) * scale_all,
        second[:channels, :hidden_count] * scale_all,
        second[channels : 2 * channels, :hidden_count] * scale_all,
        second[:hidden_count, hidden_count : hidden_count + channels] * scale_all,
    )


def solution(mesh):
    split = P(None, "tm", None, "rows", None)
    in_specs = (split, split, P(), P(), P(), P(), P(), P())
    out_specs = (split, P(None, "tm", None), P(), P(), P(), P())
    return jax.shard_map(shards, mesh=mesh, in_specs=in_specs, out_specs=out_specs, check_vma=False)
```

```python
import functools
import math

import jax
import jax.numpy as jnp
from jax import lax
from jax.experimental import pallas as pl
from jax.experimental.pallas import tpu as pltpu
from jax.sharding import PartitionSpec as P

F32 = jnp.float32
BF16 = jnp.bfloat16
LANES = 128
CORES, XS, YS, ZS = 2, 4, 4, 8

CORE_SWAP = [(i, i ^ 1) for i in range(CORES * XS)]


def x_shift(step):
    count = CORES * XS
    return [(i, (i + CORES * step) % count) for i in range(count)]


def y_shift(step):
    return [(i, i // YS * YS + (i + step) % YS) for i in range(YS * ZS)]


Z_GROUPS = [[z * YS + y for z in range(ZS)] for y in range(YS)]


def mm(a, b):
    return jnp.dot(a, b, preferred_element_type=F32)


def mm_nt(a, b):
    return lax.dot_general(a, b, (((1,), (1,)), ((), ())), preferred_element_type=F32)


def shifted(value, step):
    lane = lax.broadcasted_iota(jnp.int32, (value.shape[0], LANES), 1)
    inside = lane < LANES - 1 if step > 0 else lane > 0
    blocks = []
    for at in range(0, value.shape[1], LANES):
        rolled = pltpu.roll(value[:, at : at + LANES], (-step) % LANES, 1)
        blocks.append(jnp.where(inside, rolled, 0.0))
    return jnp.concatenate(blocks, 1)


def wide(value, width):
    return jnp.concatenate([value] * (width // LANES), 1)


def row_taps(low, x, high):
    padded = jnp.concatenate([low, x, high], 1)
    width = x.shape[1]
    return jnp.concatenate([padded[:, LANES * a : LANES * a + width] for a in range(3)], 0)


def core_select(core_ref, seq, mine_ref, other_ref, value):
    @pl.when(core_ref[0] == seq)
    def _():
        mine_ref[...] = value

    @pl.when(core_ref[0] != seq)
    def _():
        other_ref[...] = value


def conv_inner_body(keep_ref, x_ref, w_ref, gamma_ref, upd_ref, edge_ref, end_ref):
    seq = pl.program_id(0)
    frames, channels, width = x_ref.shape
    inner = width - 2 * LANES
    state = jnp.zeros((channels, inner), F32)
    nothing = jnp.zeros((channels, LANES), BF16)
    for f in range(frames):
        y = mm(w_ref[...], row_taps(nothing, x_ref[f], nothing))
        out = (
            y[channels : 2 * channels]
            + shifted(y[:channels], -1)
            + shifted(y[2 * channels :], 1)
        )
        edge_ref[f, :, :LANES] = out[:, :LANES]
        edge_ref[f, :, LANES:] = out[:, width - LANES :]
        out = out[:, LANES : width - LANES].astype(BF16)
        upd_ref[f] = out
        decay = gamma_ref[f] * keep_ref[seq * frames + f]
        state = wide(decay, inner) * state + out.astype(F32)
    end_ref[0] = state.astype(BF16)


def conv_edge_body(
    keep_ref, core_ref, low_ref, high_ref, edge_ref, inner_end_ref, w_ref, gamma_ref,
    upd_ref, mine_ref, other_ref,
):
    seq = pl.program_id(0)
    frames, channels, _ = low_ref.shape
    low = jnp.concatenate([low_ref[f] for f in range(frames)], 1)
    high = jnp.concatenate([high_ref[f] for f in range(frames)], 1)
    edges = []
    for y in (mm(w_ref[:, :channels], low), mm(w_ref[:, 2 * channels :], high)):
        edges.append(
            y[channels : 2 * channels]
            + shifted(y[:channels], -1)
            + shifted(y[2 * channels :], 1)
        )
    state = jnp.zeros((channels, 2 * LANES), F32)
    for f in range(frames):
        at = slice(f * LANES, (f + 1) * LANES)
        out = (edge_ref[f] + jnp.concatenate([edge[:, at] for edge in edges], 1)).astype(BF16)
        upd_ref[f] = out
        decay = gamma_ref[f] * keep_ref[seq * frames + f]
        state = wide(decay, 2 * LANES) * state + out.astype(F32)
    state = state.astype(BF16)
    end = jnp.concatenate([state[:, :LANES], inner_end_ref[0], state[:, LANES:]], 1)
    core_select(core_ref, seq, mine_ref, other_ref, end)


def join_weights(weights_ref):
    channels = weights_ref.shape[0] // 3
    turned = weights_ref[...].astype(F32).T.astype(BF16)
    return turned[:, : 2 * channels], turned[:, 2 * channels :]


def prior_states(keep_ref, core_ref, upd_ref, entry_ref, got_ref, gamma_ref):
    seq = pl.program_id(0)
    frames, _, width = upd_ref.shape
    state = jnp.where(core_ref[0] == seq, entry_ref[...], got_ref[...])
    for f in range(frames):
        prior = state * keep_ref[seq * frames + f]
        yield prior
        if f + 1 < frames:
            state = wide(gamma_ref[f], width) * prior + upd_ref[f].astype(F32)


def join_frame(mix, out_w, joined, og):
    preact = mm(mix, joined)
    gate = 1.0 / (1.0 + jnp.exp(-preact))
    hidden = (preact * gate).astype(BF16)
    hidden_grad = mm(out_w, og)
    pre_grad = (hidden_grad * gate * (1.0 + preact * (1.0 - gate))).astype(BF16)
    return hidden, pre_grad


def join_body(
    keep_ref, core_ref, upd_ref, x_ref, og_ref, entry_ref, got_ref, gamma_ref, weights_ref,
    mine_ref, other_ref, low_ref,
):
    seq = pl.program_id(0)
    frames, channels, width = x_ref.shape
    mix, out_w = join_weights(weights_ref)
    context_w = weights_ref[:channels]
    for f, prior in enumerate(prior_states(keep_ref, core_ref, upd_ref, entry_ref, got_ref, gamma_ref)):
        low_ref[f] = prior.astype(BF16)
    back = jnp.zeros((channels, width), F32)
    for f in reversed(range(frames)):
        joined = jnp.concatenate([low_ref[f], x_ref[f]], 0)
        _, pre_grad = join_frame(mix, out_w, joined, og_ref[f])
        prior_grad = mm(context_w, pre_grad)
        back = (wide(gamma_ref[f], width) * back + prior_grad) * keep_ref[seq * frames + f]
    core_select(core_ref, seq, mine_ref, other_ref, back.astype(BF16))


def mix_grad_body(
    keep_ref, core_ref, upd_ref, x_ref, og_ref, entry_ref, got_ref, gamma_ref, weights_ref,
    prior_ref, pgrad_ref, recon_ref, mixg_ref,
):
    seq = pl.program_id(0)
    frames, channels, _ = x_ref.shape
    mix, out_w = join_weights(weights_ref)
    total = jnp.zeros(mixg_ref.shape, F32)
    for f, prior in enumerate(prior_states(keep_ref, core_ref, upd_ref, entry_ref, got_ref, gamma_ref)):
        prior_ref[f] = prior
        joined = jnp.concatenate([prior.astype(BF16), x_ref[f]], 0)
        og = og_ref[f]
        hidden, pre_grad = join_frame(mix, out_w, joined, og)
        pgrad_ref[f] = mm(weights_ref[:channels], pre_grad)
        recon_ref[f] = mm(weights_ref[2 * channels :], hidden).astype(BF16)
        total = total + mm_nt(
            jnp.concatenate([joined, og], 0), jnp.concatenate([pre_grad, hidden], 0)
        )

    @pl.when(seq == 0)
    def _():
        mixg_ref[...] = total

    @pl.when(seq != 0)
    def _():
        mixg_ref[...] += total


def grad_body(
    keep_ref, core_ref, tm_ref, x_ref, low_ref, high_ref, prior_ref, pgrad_ref, entry_ref, got_ref,
    gamma_ref, mixg_ref, pack_ref,
):
    seq = pl.program_id(0)
    frames, channels, width = x_ref.shape
    taps_rows = 3 * channels
    half = LANES // 2
    rest = taps_rows - LANES

    @pl.when(seq == 0)
    def _():
        lane = lax.broadcasted_iota(jnp.int32, (2 * channels, LANES), 1)
        pack_ref[...] = jnp.zeros_like(pack_ref)
        pack_ref[1, : 2 * channels] = jnp.where(lane < half, mixg_ref[: 2 * channels], 0.0)
        pack_ref[1, 2 * channels : taps_rows] = jnp.where(
            lane[:channels] >= half, mixg_ref[2 * channels :], 0.0
        )

    lane = lax.broadcasted_iota(jnp.int32, (channels, LANES), 1)
    state = jnp.where(core_ref[0] == seq, entry_ref[...], got_ref[...])
    first = jnp.zeros((taps_rows, LANES), F32)
    second = jnp.zeros((taps_rows, LANES), F32)
    decay_grad = jnp.zeros((channels, LANES), F32)
    before = jnp.zeros((half, width), BF16)
    after = jnp.zeros((half - rest, width), BF16)
    for f in reversed(range(frames)):
        product = prior_ref[f] * state
        folded = product[:, :LANES]
        for at in range(LANES, width, LANES):
            folded = folded + product[:, at : at + LANES]
        column = jnp.sum(folded, axis=1, keepdims=True)
        slot = (tm_ref[0] * 2 + seq) * frames + f
        decay_grad = decay_grad + jnp.where(lane == slot, column, 0.0)
        u = jnp.concatenate(
            [shifted(state, 1).astype(BF16), state.astype(BF16), shifted(state, -1).astype(BF16)], 0
        )
        taps = row_taps(low_ref[f], x_ref[f], high_ref[f])
        first = first + mm_nt(taps, u[:LANES])
        second = second + mm_nt(taps, jnp.concatenate([before, u[LANES:], after], 0))
        state = (wide(gamma_ref[f], width) * state + pgrad_ref[f]) * keep_ref[seq * frames + f]
    pack_ref[0, :taps_rows] += first
    pack_ref[1, : 2 * channels] += second[: 2 * channels]
    pack_ref[1, :channels] += pltpu.roll(second[2 * channels :], rest, 1)
    pack_ref[1, 2 * channels : taps_rows] += decay_grad


def unpack_body(core_ref, tm_ref, mine_ref, got_ref, conv_ref, ctx_ref, feat_ref, out_t_ref, decay_ref, *, scale_all, scale_pix):
    channels, half = ctx_ref.shape
    taps_rows = 3 * channels
    rest = taps_rows - LANES
    mine = mine_ref[...]
    got = got_ref[...]
    own = core_ref[0] == 0
    first = jnp.where(own, mine, got)
    second = jnp.where(own, got, mine)
    ctx_ref[...] = second[:channels, :half] * scale_all
    feat_ref[...] = second[channels : 2 * channels, :half] * scale_all
    last = second[2 * channels : taps_rows]
    out_t_ref[...] = pltpu.roll(last, half, 1)[:, :half] * scale_all
    frames = decay_ref.shape[0]
    slots = pltpu.roll(last, LANES - tm_ref[0] * frames, 1)
    decay_ref[...] = slots.T[:frames] * scale_pix
    lane = lax.broadcasted_iota(jnp.int32, (channels, LANES), 1)
    for a in range(3):
        block = first[a * channels : (a + 1) * channels] * scale_all
        tail = second[:channels] if a == 2 else second[a * channels : (a + 1) * channels]
        at = half + (rest if a == 2 else 0)
        tail = pltpu.roll(tail * scale_all, (channels - rest - at) % LANES, 1)
        conv_ref[3 * a] = block[:, :channels]
        conv_ref[3 * a + 1] = pltpu.roll(block, LANES - channels, 1)[:, :channels]
        block = jnp.where(lane < channels - rest, pltpu.roll(block, LANES - 2 * channels, 1), tail)
        conv_ref[3 * a + 2] = block[:, :channels]


def smem():
    return pl.BlockSpec(memory_space=pltpu.SMEM)


def by_seq(shape):
    return pl.BlockSpec(shape, lambda s: (s,) + (0,) * (len(shape) - 1))


def whole(shape):
    return pl.BlockSpec(shape, lambda *_: (0,) * len(shape))


def params(mib):
    return pltpu.CompilerParams(vmem_limit_bytes=mib * 1024 * 1024)


def cost(flops, moved):
    return pl.CostEstimate(flops=flops, bytes_accessed=moved, transcendentals=0)


def exchange(mine, other, factors, reverse, beside=None):
    core = lax.axis_index("tm") % CORES
    chip = lax.axis_index("tm") // CORES
    second = core == 1
    got = lax.ppermute(other, "tm", CORE_SWAP)
    factor = jnp.where(second, factors[1], factors[0]).reshape(XS, CORES, -1)
    here = lax.dynamic_index_in_dim(factor, chip, 0, keepdims=False)
    mine_first = second if reverse else jnp.logical_not(second)
    early = jnp.where(mine_first, mine, got).astype(F32)
    late = jnp.where(mine_first, got, mine).astype(F32)
    early_factor, late_factor = (here[1], here[0]) if reverse else (here[0], here[1])
    chip_end = (late_factor[:, None] * early + late).astype(BF16)
    chip_factor = factor[:, 0] * factor[:, 1]
    came = [
        lax.ppermute(chip_end, "tm", x_shift(-step if reverse else step)) for step in range(1, XS)
    ]
    done = None
    if beside is not None:
        came, done = lax.optimization_barrier((came, beside(chip_end)))
    entry = None
    weight = jnp.ones_like(chip_factor[0])
    for step in range(1, XS):
        source = chip + step if reverse else chip - step
        there = source < XS if reverse else source >= 0
        term = jnp.where(there, weight, 0.0)[:, None] * came[step - 1].astype(F32)
        entry = term if entry is None else entry + term
        weight = weight * lax.dynamic_index_in_dim(chip_factor, source % XS, 0, keepdims=False)
    to_late = early_factor[:, None] * entry + early
    own = jnp.where(mine_first, entry, to_late)
    sent = jnp.where(mine_first, to_late, entry).astype(BF16)
    return own, lax.ppermute(sent, "tm", CORE_SWAP).astype(F32), done


def all_sum(pack, beside):
    second = lax.axis_index("tm") % CORES == 1
    mine = jnp.where(second, pack[1], pack[0])
    other = jnp.where(second, pack[0], pack[1])
    total = mine + lax.ppermute(other, "tm", CORE_SWAP)
    for axis, shift in (("tm", x_shift), ("rows", y_shift)):
        sent = total.astype(BF16)
        came = [lax.ppermute(sent, axis, shift(step)) for step in (1, 2, 3)]
        came, beside = lax.optimization_barrier((came, beside))
        came = [part.astype(F32) for part in came]
        total = (sent.astype(F32) + came[1]) + (came[0] + came[2])
    sent = jnp.broadcast_to(total.astype(BF16)[None], (ZS,) + total.shape)
    came = lax.all_to_all(sent, "rows", 0, 0, axis_index_groups=Z_GROUPS)
    mine = jnp.sum(came.astype(F32), axis=0)
    return mine, lax.ppermute(mine, "tm", CORE_SWAP), beside


def shards(
    features, out_grad, decay_rate, clip_start, conv_kernel, context_mix, feature_mix, output_mix
):
    seqs, frames, channels, rows, cols = features.shape
    tm_count = lax.axis_size("tm")
    rows_count = lax.axis_size("rows")
    all_frames = frames * tm_count
    height = rows * rows_count
    pixels = rows * cols
    inner = pixels - 2 * cols
    count = seqs * frames
    scale_all = 1.0 / math.sqrt(seqs * all_frames * height * cols)
    scale_pix = 1.0 / math.sqrt(height * cols)
    tm = lax.axis_index("tm")
    core = (tm % CORES).reshape(1)

    x = features.reshape(count, channels, pixels)
    down = [(i, i + 1) for i in range(rows_count - 1)]
    up = [(i + 1, i) for i in range(rows_count - 1)]
    low = lax.ppermute(features[:, :, :, rows - 1].reshape(count, channels, cols), "rows", down)
    high = lax.ppermute(features[:, :, :, 0].reshape(count, channels, cols), "rows", up)

    og = out_grad.reshape(count, channels, pixels)
    frame_ids = jnp.arange(all_frames, dtype=jnp.int32)
    keep_all = (frame_ids[None, :] != clip_start[:, None]).astype(F32)
    kept = (keep_all[:, :, None] * decay_rate).reshape(seqs, tm_count, frames, channels)
    factors = kept[:, :, 0]
    for f in range(1, frames):
        factors = factors * kept[:, :, f]
    keep = lax.dynamic_slice_in_dim(keep_all, tm * frames, frames, 1).reshape(-1)
    gamma = lax.dynamic_slice_in_dim(decay_rate, tm * frames, frames, 1)
    gamma = jnp.broadcast_to(gamma.reshape(count, channels, 1), (count, channels, LANES))
    taps_w = conv_kernel.reshape(3, 3, channels, channels).transpose(1, 3, 0, 2)
    taps_w = taps_w.reshape(3 * channels, 3 * channels)
    out_t = output_mix.T

    sds = jax.ShapeDtypeStruct
    xs = by_seq((frames, channels, pixels))
    ins = by_seq((frames, channels, inner))
    edges = by_seq((frames, channels, 2 * cols))
    edge = by_seq((frames, channels, cols))
    state = whole((channels, pixels))
    gs = by_seq((frames, channels, LANES))
    full = (count, channels, pixels)
    state_out = sds((channels, pixels), BF16)

    update, edge_sums, inner_end = pl.pallas_call(
        conv_inner_body,
        grid=(seqs,),
        in_specs=[smem(), xs, whole(taps_w.shape), gs],
        out_specs=[ins, edges, by_seq((1, channels, inner))],
        out_shape=[
            sds((count, channels, inner), BF16),
            sds((count, channels, 2 * cols), F32),
            sds((seqs, channels, inner), BF16),
        ],
        compiler_params=params(16),
        cost_estimate=cost(340_000_000, 2_000_000),
        name="conv_inner",
    )(keep, x, taps_w, gamma)

    edge_update, mine, other = pl.pallas_call(
        conv_edge_body,
        grid=(seqs,),
        in_specs=[
            smem(), smem(), edge, edge, edges, by_seq((1, channels, inner)), whole(taps_w.shape), gs,
        ],
        out_specs=[edges, state, state],
        out_shape=[sds((count, channels, 2 * cols), BF16), state_out, state_out],
        compiler_params=params(16),
        cost_estimate=cost(30_000_000, 2_000_000),
        name="conv_edge",
    )(keep, core, low, high, edge_sums, inner_end, taps_w, gamma)

    update = jnp.concatenate(
        [edge_update[:, :, :cols], update, edge_update[:, :, cols:]], axis=2
    )
    entry, entry_got, _ = exchange(mine, other, factors, False)

    weights = jnp.concatenate([context_mix, feature_mix, out_t], 0)
    mix = whole(context_mix.shape)
    join_in = (keep, core, update, x, og, entry, entry_got, gamma, weights)
    join_specs = [smem(), smem(), xs, xs, xs, state, state, gs, whole(weights.shape)]
    mine, other = pl.pallas_call(
        join_body,
        grid=(seqs,),
        in_specs=join_specs,
        out_specs=[state, state],
        out_shape=[state_out, state_out],
        scratch_shapes=[pltpu.VMEM((frames, channels, pixels), BF16)],
        compiler_params=params(24),
        cost_estimate=cost(300_000_000, 3_000_000),
        name="join",
    )(*join_in)

    mixg_shape = (3 * channels, LANES)

    def mix_grad(chip_end):
        late_entry, _ = lax.optimization_barrier((entry, chip_end))
        return pl.pallas_call(
            mix_grad_body,
            grid=(seqs,),
            in_specs=join_specs,
            out_specs=[xs, xs, xs, whole(mixg_shape)],
            out_shape=[sds(full, F32), sds(full, F32), sds(full, BF16), sds(mixg_shape, F32)],
            compiler_params=params(24),
            cost_estimate=cost(600_000_000, 8_000_000),
            name="mix_grad",
        )(*join_in[:5], late_entry, *join_in[6:])

    back, back_got, (priors, prior_grads, recon, mixg) = exchange(
        mine, other, factors, True, mix_grad
    )
    recon = recon.reshape(features.shape)

    pack_shape = (2, 3 * channels, LANES)
    pack = pl.pallas_call(
        grad_body,
        grid=(seqs,),
        in_specs=[
            smem(), smem(), smem(), xs, edge, edge, xs, xs, state, state, gs, whole(mixg_shape),
        ],
        out_specs=whole(pack_shape),
        out_shape=sds(pack_shape, F32),
        compiler_params=params(24),
        cost_estimate=cost(340_000_000, 8_000_000),
        name="grad",
    )(keep, core, tm.reshape(1), x, low, high, priors, prior_grads, back, back_got, gamma, mixg)

    mine, got, recon = all_sum(pack, recon)
    taps_grad, ctx_grad, feat_grad, out_grad_t, decay_grad = pl.pallas_call(
        functools.partial(unpack_body, scale_all=scale_all, scale_pix=scale_pix),
        in_specs=[smem(), smem(), whole(mine.shape), whole(mine.shape)],
        out_specs=[
            whole((9, channels, channels)), mix, mix, mix, whole((count, channels)),
        ],
        out_shape=[
            sds((9, channels, channels), F32),
            sds(context_mix.shape, F32), sds(context_mix.shape, F32), sds(out_t.shape, F32),
            sds((count, channels), F32),
        ],
        compiler_params=params(4),
        name="unpack",
    )(core, tm.reshape(1), mine, got)
    return (
        recon,
        decay_grad.reshape(seqs, frames, channels),
        taps_grad,
        ctx_grad,
        feat_grad,
        out_grad_t.T,
    )


def solution(mesh):
    split = P(None, "tm", None, "rows", None)
    in_specs = (split, split, P(), P(), P(), P(), P(), P())
    out_specs = (split, P(None, "tm", None), P(), P(), P(), P())
    return jax.shard_map(shards, mesh=mesh, in_specs=in_specs, out_specs=out_specs, check_vma=False)
```

```python
import functools
import math

import jax
import jax.numpy as jnp
from jax import lax
from jax.experimental import pallas as pl
from jax.experimental.pallas import tpu as pltpu
from jax.sharding import PartitionSpec as P

F32 = jnp.float32
BF16 = jnp.bfloat16
LANES = 128
CORES, XS, YS, ZS = 2, 4, 4, 8

CORE_SWAP = [(i, i ^ 1) for i in range(CORES * XS)]


def row_swap(first):
    pairs = [(i, i + 1) for i in range(first, YS * ZS - 1, 2)]
    return pairs + [(j, i) for i, j in pairs]


def x_shift(step):
    count = CORES * XS
    return [(i, (i + CORES * step) % count) for i in range(count)]


def y_shift(step):
    return [(i, i // YS * YS + (i + step) % YS) for i in range(YS * ZS)]


Z_GROUPS = [[z * YS + y for z in range(ZS)] for y in range(YS)]


def mm(a, b):
    return jnp.dot(a, b, preferred_element_type=F32)


def mm_nt(a, b):
    return lax.dot_general(a, b, (((1,), (1,)), ((), ())), preferred_element_type=F32)


def shifted(value, step):
    lane = lax.broadcasted_iota(jnp.int32, (value.shape[0], LANES), 1)
    inside = lane < LANES - 1 if step > 0 else lane > 0
    blocks = []
    for at in range(0, value.shape[1], LANES):
        rolled = pltpu.roll(value[:, at : at + LANES], (-step) % LANES, 1)
        blocks.append(jnp.where(inside, rolled, 0.0))
    return jnp.concatenate(blocks, 1)


def wide(value, width):
    return jnp.concatenate([value] * (width // LANES), 1)


def row_taps(low, x, high):
    padded = jnp.concatenate([low, x, high], 1)
    width = x.shape[1]
    return jnp.concatenate([padded[:, LANES * a : LANES * a + width] for a in range(3)], 0)


def place():
    tm = lax.axis_index("tm")
    return tm // CORES, lax.rem(tm, CORES)


def halos(halo_ref, got_ref, f, frames):
    _, core = place()
    odd = lax.rem(lax.axis_index("rows"), 2)
    own = halo_ref.shape[2]
    at = f % own
    mine_first = core == 0 if f < own else core == 1
    return [
        jnp.where(mine_first, halo_ref[side, core, at], got_ref[side, at]) for side in (1 - odd, odd)
    ]


def conv_body(
    clip_ref, x_ref, halo_ref, got_ref, w_ref, decay_ref, upd_ref, end_ref, table_ref, keep_ref
):
    frames, channels, width = x_ref.shape
    chip, core = place()
    rates = decay_ref[core, pl.ds(pl.multiple_of(chip * frames, frames), frames)].T
    middle = []
    for at in range(1, XS - 1):
        product = None
        for f in range(at * frames, (at + 1) * frames):
            kept = jnp.where(clip_ref[core] == f, 0.0, 1.0) * decay_ref[core, f : f + 1]
            product = kept if product is None else product * kept
        middle.append(jnp.broadcast_to(product.T, (channels, LANES)))
    ones = jnp.ones((channels, LANES), F32)
    nought = jnp.zeros((channels, LANES), F32)
    both = middle[0] * middle[1]
    for at, weight in enumerate(
        [
            jnp.where(chip >= 1, ones, nought),
            jnp.where(chip == 2, middle[0], jnp.where(chip == 3, middle[1], nought)),
            jnp.where(chip == 3, both, nought),
            jnp.where(chip <= 2, ones, nought),
            jnp.where(chip == 0, middle[0], jnp.where(chip == 1, middle[1], nought)),
            jnp.where(chip == 0, both, nought),
        ]
    ):
        table_ref[frames + at] = weight
    state = jnp.zeros((channels, width), F32)
    for f in range(frames):
        gamma = jnp.broadcast_to(rates[:, f : f + 1], (channels, LANES))
        table_ref[f] = gamma
        keep = jnp.where(clip_ref[core] == chip * frames + f, 0.0, 1.0).astype(F32)
        keep_ref[f] = jnp.broadcast_to(keep, keep_ref.shape[1:])
        low, high = halos(halo_ref, got_ref, f, frames)
        y = mm(w_ref[...], row_taps(low, x_ref[f], high))
        out = (
            y[channels : 2 * channels]
            + shifted(y[:channels], -1)
            + shifted(y[2 * channels :], 1)
        ).astype(BF16)
        upd_ref[f] = out
        state = wide(gamma * keep, width) * state + out.astype(F32)
    end_ref[...] = state.astype(BF16)


def kept(keep_ref, f, value):
    rows, width = value.shape
    tile = jnp.concatenate([keep_ref[f]] * (rows // keep_ref.shape[1]), 0)
    return value * wide(tile, width)


GROUP = 4


def blocks(weight):
    blank = jnp.zeros_like(weight)
    return jnp.concatenate(
        [
            jnp.concatenate([weight if i == j else blank for j in range(GROUP)], 1)
            for i in range(GROUP)
        ],
        0,
    )


def join_weights(weights_ref):
    channels = weights_ref.shape[0] // 3
    turned = weights_ref[...].astype(F32).T
    row = lax.broadcasted_iota(jnp.int32, turned.shape, 1) < 2 * channels
    mix = jnp.concatenate([jnp.where(row, turned, 0.0), jnp.where(row, 0.0, turned)], 0)
    return mix.astype(BF16), blocks(weights_ref[:channels]), blocks(weights_ref[2 * channels :])


def entering(came_refs, table_ref, first):
    state = None
    for at, ref in enumerate(came_refs):
        term = wide(table_ref[first + at], ref.shape[1]) * ref[...].astype(F32)
        state = term if state is None else state + term
    return state


def prior_states(keep_ref, upd_ref, came_refs, table_ref):
    frames, _, width = upd_ref.shape
    state = entering(came_refs, table_ref, frames)
    for f in range(frames):
        prior = kept(keep_ref, f, state)
        yield prior
        if f + 1 < frames:
            state = wide(table_ref[f], width) * prior + upd_ref[f].astype(F32)


def gates(preact, hidden_grad):
    gate = 0.5 * jnp.tanh(0.5 * preact) + 0.5
    pre_grad = (hidden_grad * gate * (1.0 + preact * (1.0 - gate))).astype(BF16)
    return gate, pre_grad


def join_body(
    upd_ref, x_ref, og_ref, came1_ref, came2_ref, came3_ref, table_ref, keep_ref, weights_ref,
    end_ref, low_ref,
):
    frames, channels, width = x_ref.shape
    hidden_count = weights_ref.shape[1]
    mix, ctx, _ = join_weights(weights_ref)
    came = (came1_ref, came2_ref, came3_ref)
    for f, prior in enumerate(prior_states(keep_ref, upd_ref, came, table_ref)):
        low_ref[f] = prior.astype(BF16)
    back = jnp.zeros((channels, width), F32)
    for f in reversed(range(0, frames, GROUP)):
        pre_grads = []
        for i in range(f, f + GROUP):
            both = mm(mix, jnp.concatenate([low_ref[i], x_ref[i], og_ref[i]], 0))
            pre_grads.append(gates(both[:hidden_count], both[hidden_count:])[1])
        prior_grad = mm(ctx, jnp.concatenate(pre_grads, 0))
        for i in reversed(range(GROUP)):
            grad = prior_grad[i * channels : (i + 1) * channels]
            back = kept(keep_ref, f + i, wide(table_ref[f + i], width) * back + grad)
    end_ref[...] = back.astype(BF16)


def mix_grad_body(
    upd_ref, x_ref, og_ref, came1_ref, came2_ref, came3_ref, table_ref, keep_ref, weights_ref,
    prior_ref, pgrad_ref, recon_ref, mixg_ref,
):
    channels = x_ref.shape[1]
    hidden_count = weights_ref.shape[1]
    mix, ctx, out_t = join_weights(weights_ref)
    came = (came1_ref, came2_ref, came3_ref)
    total = jnp.zeros(mixg_ref.shape, F32)
    hiddens, pre_grads = [], []
    for f, prior in enumerate(prior_states(keep_ref, upd_ref, came, table_ref)):
        prior_ref[f] = prior
        joined = jnp.concatenate([prior.astype(BF16), x_ref[f], og_ref[f]], 0)
        both = mm(mix, joined)
        preact = both[:hidden_count]
        gate, pre_grad = gates(preact, both[hidden_count:])
        hiddens.append((preact * gate).astype(BF16))
        pre_grads.append(pre_grad)
        total = total + mm_nt(joined, jnp.concatenate([pre_grad, hiddens[-1]], 0))
        if len(hiddens) < GROUP:
            continue
        prior_grad = mm(ctx, jnp.concatenate(pre_grads, 0))
        recon = mm(out_t, jnp.concatenate(hiddens, 0)).astype(BF16)
        for i in range(GROUP):
            pgrad_ref[f + 1 - GROUP + i] = prior_grad[i * channels : (i + 1) * channels]
            recon_ref[f + 1 - GROUP + i] = recon[i * channels : (i + 1) * channels]
        hiddens, pre_grads = [], []
    mixg_ref[...] = total


def grad_body(
    x_ref, halo_ref, got_ref, prior_ref, pgrad_ref, came1_ref, came2_ref, came3_ref, table_ref,
    keep_ref, mixg_ref, pack_ref,
):
    frames, channels, width = x_ref.shape
    taps_rows = 3 * channels
    half = LANES // 2
    rest = taps_rows - LANES
    chip, core = place()
    lane = lax.broadcasted_iota(jnp.int32, (channels, LANES), 1)
    state = entering((came1_ref, came2_ref, came3_ref), table_ref, frames + XS - 1)
    total = jnp.zeros((taps_rows, taps_rows), F32)
    decay_grad = jnp.zeros((channels, LANES), F32)
    for f in reversed(range(frames)):
        product = prior_ref[f] * state
        folded = product[:, :LANES]
        for at in range(LANES, width, LANES):
            folded = folded + product[:, at : at + LANES]
        column = jnp.sum(folded, axis=1, keepdims=True)
        slot = (chip * CORES + core) * frames + f
        decay_grad = decay_grad + jnp.where(lane == slot, column, 0.0)
        u = jnp.concatenate(
            [shifted(state, 1).astype(BF16), state.astype(BF16), shifted(state, -1).astype(BF16)], 0
        )
        low, high = halos(halo_ref, got_ref, f, frames)
        taps = row_taps(low, x_ref[f], high)
        total = total + mm_nt(taps, u)
        if f:
            state = kept(keep_ref, f, wide(table_ref[f], width) * state + pgrad_ref[f])
    pack_ref[0] = total[:, :LANES]
    second = jnp.concatenate([total[:, LANES:], jnp.zeros((taps_rows, LANES - rest), F32)], 1)
    second = pltpu.roll(second, half, 1)
    wide_lane = lax.broadcasted_iota(jnp.int32, (2 * channels, LANES), 1)
    pack_ref[1, : 2 * channels] = second[: 2 * channels] + jnp.where(
        wide_lane < half, mixg_ref[: 2 * channels], 0.0
    )
    pack_ref[1, :channels] += pltpu.roll(second[2 * channels :], rest, 1)
    pack_ref[1, 2 * channels :] = decay_grad + jnp.where(lane >= half, mixg_ref[2 * channels :], 0.0)


def unpack_body(mine_ref, got_ref, conv_ref, ctx_ref, feat_ref, out_t_ref, decay_ref, *, scale_all, scale_pix):
    channels, half = ctx_ref.shape
    taps_rows = 3 * channels
    rest = taps_rows - LANES
    chip, core = place()
    mine = mine_ref[...]
    got = got_ref[...]
    first = jnp.where(core == 0, mine, got)
    second = jnp.where(core == 0, got, mine)
    ctx_ref[...] = second[:channels, :half] * scale_all
    feat_ref[...] = second[channels : 2 * channels, :half] * scale_all
    last = second[2 * channels : taps_rows]
    out_t_ref[...] = pltpu.roll(last, half, 1)[:, :half] * scale_all
    seqs, frames, _ = decay_ref.shape
    first_lane = (chip * seqs * CORES + core) * frames
    slots = pltpu.roll(last, LANES - first_lane, 1).T * scale_pix
    for s in range(seqs):
        decay_ref[s] = slots[s * CORES * frames : s * CORES * frames + frames]
    lane = lax.broadcasted_iota(jnp.int32, (channels, LANES), 1)
    for a in range(3):
        block = first[a * channels : (a + 1) * channels] * scale_all
        tail = second[:channels] if a == 2 else second[a * channels : (a + 1) * channels]
        at = half + (rest if a == 2 else 0)
        tail = pltpu.roll(tail * scale_all, (channels - rest - at) % LANES, 1)
        conv_ref[3 * a] = block[:, :channels]
        conv_ref[3 * a + 1] = pltpu.roll(block, LANES - channels, 1)[:, :channels]
        block = jnp.where(lane < channels - rest, pltpu.roll(block, LANES - 2 * channels, 1), tail)
        conv_ref[3 * a + 2] = block[:, :channels]


def smem():
    return pl.BlockSpec(memory_space=pltpu.SMEM)


def kernel(body, name, operands, outs, flops, scratch=(), mib=16):
    specs = [smem() if value.ndim == 1 else pl.BlockSpec(value.shape, lambda n=value.ndim: (0,) * n) for value in operands]
    moved = sum(math.prod(value.shape) * value.dtype.itemsize for value in (*operands, *outs))
    return pl.pallas_call(
        body,
        in_specs=specs,
        out_specs=[pl.BlockSpec(out.shape, lambda n=out.ndim: (0,) * n) for out in outs],
        out_shape=outs,
        scratch_shapes=scratch,
        compiler_params=pltpu.CompilerParams(vmem_limit_bytes=mib * 1024 * 1024),
        cost_estimate=pl.CostEstimate(flops=flops, bytes_accessed=moved, transcendentals=0),
        name=name,
    )(*operands)


def exchange(chip_end, reverse, beside=None):
    came = [
        lax.ppermute(chip_end, "tm", x_shift(-step if reverse else step)) for step in range(1, XS)
    ]
    if beside is None:
        return came
    return lax.optimization_barrier((tuple(came), beside(chip_end)))


def own_frames(mine, got):
    early = place()[1] == 0
    return jnp.concatenate([jnp.where(early, mine, got), jnp.where(early, got, mine)], 0)


def all_sum(pack, recon):
    core = place()[1]
    second = core == 1
    mine = jnp.where(second, pack[1], pack[0])
    other = jnp.where(second, pack[0], pack[1])
    total = mine + lax.ppermute(other, "tm", CORE_SWAP)
    total, recon = lax.optimization_barrier((total, recon))
    frames = recon.shape[0] // CORES
    kept = jnp.where(second, recon[frames:], recon[:frames])
    got = lax.ppermute(jnp.where(second, recon[:frames], recon[frames:]), "tm", CORE_SWAP)
    beside = [
        (kept, got),
        lambda kept, got: jnp.stack(
            [jnp.where(second, got, kept), jnp.where(second, kept, got)], 0
        ).reshape(2, frames, recon.shape[1], -1, LANES),
    ]
    for axis, shift in (("tm", x_shift), ("rows", y_shift)):
        sent = total.astype(BF16)
        came = [lax.ppermute(sent, axis, shift(step)) for step in (1, 2, 3)]
        done = beside[0] if axis == "tm" else beside[1](*beside[0])
        came, done = lax.optimization_barrier((came, done))
        beside[0] = done
        came = [part.astype(F32) for part in came]
        total = (sent.astype(F32) + came[1]) + (came[0] + came[2])
    sent = jnp.broadcast_to(total.astype(BF16)[None], (ZS,) + total.shape)
    came = lax.all_to_all(sent, "rows", 0, 0, axis_index_groups=Z_GROUPS)
    mine = jnp.sum(came.astype(F32), axis=0)
    return mine, lax.ppermute(mine, "tm", CORE_SWAP), beside[0]


def shards(
    features, out_grad, decay_rate, clip_start, conv_kernel, context_mix, feature_mix, output_mix
):
    seqs, frames, channels, rows, cols = features.shape
    rows_count = lax.axis_size("rows")
    all_frames = frames * lax.axis_size("tm")
    height = rows * rows_count
    pixels = rows * cols
    count = CORES * frames
    scale_all = 1.0 / math.sqrt(seqs * all_frames * height * cols)
    scale_pix = 1.0 / math.sqrt(height * cols)
    chip, core = place()

    second = core == 1

    def share(array):
        mine = jnp.where(second, array[1], array[0])
        return mine, lax.ppermute(jnp.where(second, array[0], array[1]), "tm", CORE_SWAP)

    odd = lax.axis_index("rows") % 2 == 1
    last, first = features[:, :, :, rows - 1], features[:, :, :, 0]
    inner = lax.ppermute(jnp.where(odd, first, last), "rows", row_swap(0))
    outer = lax.ppermute(jnp.where(odd, last, first), "rows", row_swap(1))
    weights = jnp.concatenate([context_mix, feature_mix, output_mix.T], 0)
    x = own_frames(*share(features)).reshape(count, channels, pixels)
    og = own_frames(*share(out_grad)).reshape(count, channels, pixels)
    (inner, outer), (x, og, weights) = lax.optimization_barrier(((inner, outer), (x, og, weights)))
    halo = jnp.stack([inner, outer], 0)
    got = lax.ppermute(jnp.where(second, halo[:, 0], halo[:, 1]), "tm", CORE_SWAP)

    taps_w = conv_kernel.reshape(3, 3, channels, channels).transpose(1, 3, 0, 2)
    taps_w = taps_w.reshape(3 * channels, 3 * channels)
    sds = jax.ShapeDtypeStruct
    full = (count, channels, pixels)
    state = sds((channels, pixels), BF16)

    update, chip_end, table, keep = kernel(
        conv_body,
        "conv",
        (clip_start, x, halo, got, taps_w, decay_rate),
        [
            sds(full, BF16),
            state,
            sds((count + 2 * (XS - 1), channels, LANES), F32),
            sds((count, 8, LANES), F32),
        ],
        340_000_000,
    )

    came = exchange(chip_end, False)
    operands = (update, x, og, *came, table, keep, weights)
    (chip_end,) = kernel(
        join_body, "join", operands, [state], 200_000_000, [pltpu.VMEM(full, BF16)]
    )

    def mix_grad(chip_end):
        late, _ = lax.optimization_barrier((table, chip_end))
        return kernel(
            mix_grad_body,
            "mix_grad",
            (*operands[:6], late, *operands[7:]),
            [sds(full, F32), sds(full, F32), sds(full, BF16), sds((3 * channels, LANES), F32)],
            600_000_000,
        )

    came, (priors, prior_grads, recon, mixg) = exchange(chip_end, True, mix_grad)
    (pack,) = kernel(
        grad_body,
        "grad",
        (x, halo, got, priors, prior_grads, *came, table, keep, mixg),
        [sds((2, 3 * channels, LANES), F32)],
        340_000_000,
    )
    mine, got, recon = all_sum(pack, recon)
    taps_grad, ctx_grad, feat_grad, out_grad_t, decay_grad = kernel(
        functools.partial(unpack_body, scale_all=scale_all, scale_pix=scale_pix),
        "unpack",
        (mine, got),
        [
            sds((9, channels, channels), F32),
            sds(context_mix.shape, F32), sds(context_mix.shape, F32), sds(context_mix.shape, F32),
            sds((seqs, frames, channels), F32),
        ],
        1_000_000,
        mib=8,
    )
    return recon, decay_grad, taps_grad, ctx_grad, feat_grad, out_grad_t.T


def solution(mesh):
    split = P(None, "tm", None, "rows", None)
    in_specs = (split, split, P(), P(), P(), P(), P(), P())
    out_specs = (split, P(None, "tm", None), P(), P(), P(), P())
    return jax.shard_map(shards, mesh=mesh, in_specs=in_specs, out_specs=out_specs, check_vma=False)
```

```python
import functools
import math

import jax
import jax.numpy as jnp
from jax import lax
from jax.experimental import pallas as pl
from jax.experimental.pallas import tpu as pltpu
from jax.sharding import PartitionSpec as P

F32 = jnp.float32
BF16 = jnp.bfloat16
LANES = 128
CORES, XS, YS, ZS = 2, 4, 4, 8

CORE_SWAP = [(i, i ^ 1) for i in range(CORES * XS)]


def row_swap(first):
    pairs = [(i, i + 1) for i in range(first, YS * ZS - 1, 2)]
    return pairs + [(j, i) for i, j in pairs]


def x_shift(step):
    count = CORES * XS
    return [(i, (i + CORES * step) % count) for i in range(count)]


def y_shift(step):
    return [(i, i // YS * YS + (i + step) % YS) for i in range(YS * ZS)]


Z_GROUPS = [[z * YS + y for z in range(ZS)] for y in range(YS)]


def mm(a, b):
    return jnp.dot(a, b, preferred_element_type=F32)


def mm_nt(a, b):
    return lax.dot_general(a, b, (((1,), (1,)), ((), ())), preferred_element_type=F32)


def shifted(value, step):
    lane = lax.broadcasted_iota(jnp.int32, (value.shape[0], LANES), 1)
    inside = lane < LANES - 1 if step > 0 else lane > 0
    blocks = []
    for at in range(0, value.shape[1], LANES):
        rolled = pltpu.roll(value[:, at : at + LANES], (-step) % LANES, 1)
        blocks.append(jnp.where(inside, rolled, 0.0))
    return jnp.concatenate(blocks, 1)


def wide(value, width):
    return jnp.concatenate([value] * (width // LANES), 1)


def row_taps(low, x, high):
    padded = jnp.concatenate([low, x, high], 1)
    width = x.shape[1]
    return jnp.concatenate([padded[:, LANES * a : LANES * a + width] for a in range(3)], 0)


def place():
    tm = lax.axis_index("tm")
    return tm // CORES, lax.rem(tm, CORES)


def halos(halo_ref, got_ref, f, frames):
    _, core = place()
    odd = lax.rem(lax.axis_index("rows"), 2)
    own = halo_ref.shape[2]
    at = f % own
    mine_first = core == 0 if f < own else core == 1
    return [
        jnp.where(mine_first, halo_ref[side, core, at], got_ref[side, at]) for side in (1 - odd, odd)
    ]


def cut_body(features_ref, inner_ref, outer_ref, share_ref):
    _, core = place()
    even = lax.rem(lax.axis_index("rows"), 2) == 0
    seqs, frames, _, rows, _ = features_ref.shape
    for s in range(seqs):
        for f in range(frames):
            value = features_ref[s, f].astype(F32)
            first, last = value[:, 0].astype(BF16), value[:, rows - 1].astype(BF16)
            inner_ref[s, f] = jnp.where(even, last, first)
            outer_ref[s, f] = jnp.where(even, first, last)
    for f in range(frames):
        share_ref[f] = features_ref[1 - core, f]


def conv_body(
    clip_ref, x_ref, halo_ref, got_ref, w_ref, decay_ref, upd_ref, end_ref, table_ref, keep_ref
):
    frames, channels, width = x_ref.shape
    chip, core = place()
    rates = decay_ref[core, pl.ds(pl.multiple_of(chip * frames, frames), frames)].T
    middle = []
    for at in range(1, XS - 1):
        product = None
        for f in range(at * frames, (at + 1) * frames):
            kept = jnp.where(clip_ref[core] == f, 0.0, 1.0) * decay_ref[core, f : f + 1]
            product = kept if product is None else product * kept
        middle.append(jnp.broadcast_to(product.T, (channels, LANES)))
    ones = jnp.ones((channels, LANES), F32)
    nought = jnp.zeros((channels, LANES), F32)
    both = middle[0] * middle[1]
    for at, weight in enumerate(
        [
            jnp.where(chip >= 1, ones, nought),
            jnp.where(chip == 2, middle[0], jnp.where(chip == 3, middle[1], nought)),
            jnp.where(chip == 3, both, nought),
            jnp.where(chip <= 2, ones, nought),
            jnp.where(chip == 0, middle[0], jnp.where(chip == 1, middle[1], nought)),
            jnp.where(chip == 0, both, nought),
        ]
    ):
        table_ref[frames + at] = weight
    state = jnp.zeros((channels, width), F32)
    for f in range(frames):
        gamma = jnp.broadcast_to(rates[:, f : f + 1], (channels, LANES))
        table_ref[f] = gamma
        keep = jnp.where(clip_ref[core] == chip * frames + f, 0.0, 1.0).astype(F32)
        keep_ref[f] = jnp.broadcast_to(keep, keep_ref.shape[1:])
        low, high = halos(halo_ref, got_ref, f, frames)
        y = mm(w_ref[...], row_taps(low, x_ref[f], high))
        out = (
            y[channels : 2 * channels]
            + shifted(y[:channels], -1)
            + shifted(y[2 * channels :], 1)
        ).astype(BF16)
        upd_ref[f] = out
        state = wide(gamma * keep, width) * state + out.astype(F32)
    end_ref[...] = state.astype(BF16)


def kept(keep_ref, f, value):
    rows, width = value.shape
    tile = jnp.concatenate([keep_ref[f]] * (rows // keep_ref.shape[1]), 0)
    return value * wide(tile, width)


GROUP = 4


def blocks(weight):
    blank = jnp.zeros_like(weight)
    return jnp.concatenate(
        [
            jnp.concatenate([weight if i == j else blank for j in range(GROUP)], 1)
            for i in range(GROUP)
        ],
        0,
    )


def join_weights(weights_ref):
    channels = weights_ref.shape[0] // 3
    turned = weights_ref[...].astype(F32).T
    row = lax.broadcasted_iota(jnp.int32, turned.shape, 1) < 2 * channels
    mix = jnp.concatenate([jnp.where(row, turned, 0.0), jnp.where(row, 0.0, turned)], 0)
    return mix.astype(BF16), blocks(weights_ref[:channels]), blocks(weights_ref[2 * channels :])


def entering(came_refs, table_ref, first):
    state = None
    for at, ref in enumerate(came_refs):
        term = wide(table_ref[first + at], ref.shape[1]) * ref[...].astype(F32)
        state = term if state is None else state + term
    return state


def prior_states(keep_ref, upd_ref, came_refs, table_ref):
    frames, _, width = upd_ref.shape
    state = entering(came_refs, table_ref, frames)
    for f in range(frames):
        prior = kept(keep_ref, f, state)
        yield prior
        if f + 1 < frames:
            state = wide(table_ref[f], width) * prior + upd_ref[f].astype(F32)


def gates(preact, hidden_grad):
    gate = 0.5 * jnp.tanh(0.5 * preact) + 0.5
    pre_grad = (hidden_grad * gate * (1.0 + preact * (1.0 - gate))).astype(BF16)
    return gate, pre_grad


def join_body(
    upd_ref, x_ref, og_ref, came1_ref, came2_ref, came3_ref, table_ref, keep_ref, weights_ref,
    end_ref, low_ref,
):
    frames, channels, width = x_ref.shape
    hidden_count = weights_ref.shape[1]
    mix, ctx, _ = join_weights(weights_ref)
    came = (came1_ref, came2_ref, came3_ref)
    for f, prior in enumerate(prior_states(keep_ref, upd_ref, came, table_ref)):
        low_ref[f] = prior.astype(BF16)
    back = jnp.zeros((channels, width), F32)
    for f in reversed(range(0, frames, GROUP)):
        pre_grads = []
        for i in range(f, f + GROUP):
            both = mm(mix, jnp.concatenate([low_ref[i], x_ref[i], og_ref[i]], 0))
            pre_grads.append(gates(both[:hidden_count], both[hidden_count:])[1])
        prior_grad = mm(ctx, jnp.concatenate(pre_grads, 0))
        for i in reversed(range(GROUP)):
            grad = prior_grad[i * channels : (i + 1) * channels]
            back = kept(keep_ref, f + i, wide(table_ref[f + i], width) * back + grad)
    end_ref[...] = back.astype(BF16)


def mix_grad_body(
    upd_ref, x_ref, og_ref, came1_ref, came2_ref, came3_ref, table_ref, keep_ref, weights_ref,
    prior_ref, pgrad_ref, recon_ref, mixg_ref,
):
    channels = x_ref.shape[1]
    hidden_count = weights_ref.shape[1]
    mix, ctx, out_t = join_weights(weights_ref)
    came = (came1_ref, came2_ref, came3_ref)
    total = jnp.zeros(mixg_ref.shape, F32)
    hiddens, pre_grads = [], []
    for f, prior in enumerate(prior_states(keep_ref, upd_ref, came, table_ref)):
        prior_ref[f] = prior
        joined = jnp.concatenate([prior.astype(BF16), x_ref[f], og_ref[f]], 0)
        both = mm(mix, joined)
        preact = both[:hidden_count]
        gate, pre_grad = gates(preact, both[hidden_count:])
        hiddens.append((preact * gate).astype(BF16))
        pre_grads.append(pre_grad)
        total = total + mm_nt(joined, jnp.concatenate([pre_grad, hiddens[-1]], 0))
        if len(hiddens) < GROUP:
            continue
        prior_grad = mm(ctx, jnp.concatenate(pre_grads, 0))
        recon = mm(out_t, jnp.concatenate(hiddens, 0)).astype(BF16)
        for i in range(GROUP):
            pgrad_ref[f + 1 - GROUP + i] = prior_grad[i * channels : (i + 1) * channels]
            recon_ref[f + 1 - GROUP + i] = recon[i * channels : (i + 1) * channels]
        hiddens, pre_grads = [], []
    mixg_ref[...] = total


def grad_body(
    x_ref, halo_ref, got_ref, prior_ref, pgrad_ref, came1_ref, came2_ref, came3_ref, table_ref,
    keep_ref, mixg_ref, pack_ref,
):
    frames, channels, width = x_ref.shape
    taps_rows = 3 * channels
    half = LANES // 2
    rest = taps_rows - LANES
    chip, core = place()
    lane = lax.broadcasted_iota(jnp.int32, (channels, LANES), 1)
    state = entering((came1_ref, came2_ref, came3_ref), table_ref, frames + XS - 1)
    total = jnp.zeros((taps_rows, taps_rows), F32)
    decay_grad = jnp.zeros((channels, LANES), F32)
    for f in reversed(range(frames)):
        product = prior_ref[f] * state
        folded = product[:, :LANES]
        for at in range(LANES, width, LANES):
            folded = folded + product[:, at : at + LANES]
        column = jnp.sum(folded, axis=1, keepdims=True)
        slot = (chip * CORES + core) * frames + f
        decay_grad = decay_grad + jnp.where(lane == slot, column, 0.0)
        u = jnp.concatenate(
            [shifted(state, 1).astype(BF16), state.astype(BF16), shifted(state, -1).astype(BF16)], 0
        )
        low, high = halos(halo_ref, got_ref, f, frames)
        taps = row_taps(low, x_ref[f], high)
        total = total + mm_nt(taps, u)
        if f:
            state = kept(keep_ref, f, wide(table_ref[f], width) * state + pgrad_ref[f])
    pack_ref[0] = total[:, :LANES]
    second = jnp.concatenate([total[:, LANES:], jnp.zeros((taps_rows, LANES - rest), F32)], 1)
    second = pltpu.roll(second, half, 1)
    wide_lane = lax.broadcasted_iota(jnp.int32, (2 * channels, LANES), 1)
    pack_ref[1, : 2 * channels] = second[: 2 * channels] + jnp.where(
        wide_lane < half, mixg_ref[: 2 * channels], 0.0
    )
    pack_ref[1, :channels] += pltpu.roll(second[2 * channels :], rest, 1)
    pack_ref[1, 2 * channels :] = decay_grad + jnp.where(lane >= half, mixg_ref[2 * channels :], 0.0)


def unpack_body(mine_ref, got_ref, conv_ref, ctx_ref, feat_ref, out_t_ref, decay_ref, *, scale_all, scale_pix):
    channels, half = ctx_ref.shape
    taps_rows = 3 * channels
    rest = taps_rows - LANES
    chip, core = place()
    mine = mine_ref[...]
    got = got_ref[...]
    first = jnp.where(core == 0, mine, got)
    second = jnp.where(core == 0, got, mine)
    ctx_ref[...] = second[:channels, :half] * scale_all
    feat_ref[...] = second[channels : 2 * channels, :half] * scale_all
    last = second[2 * channels : taps_rows]
    out_t_ref[...] = pltpu.roll(last, half, 1)[:, :half] * scale_all
    seqs, frames, _ = decay_ref.shape
    first_lane = (chip * seqs * CORES + core) * frames
    slots = pltpu.roll(last, LANES - first_lane, 1).T * scale_pix
    for s in range(seqs):
        decay_ref[s] = slots[s * CORES * frames : s * CORES * frames + frames]
    lane = lax.broadcasted_iota(jnp.int32, (channels, LANES), 1)
    for a in range(3):
        block = first[a * channels : (a + 1) * channels] * scale_all
        tail = second[:channels] if a == 2 else second[a * channels : (a + 1) * channels]
        at = half + (rest if a == 2 else 0)
        tail = pltpu.roll(tail * scale_all, (channels - rest - at) % LANES, 1)
        conv_ref[3 * a] = block[:, :channels]
        conv_ref[3 * a + 1] = pltpu.roll(block, LANES - channels, 1)[:, :channels]
        block = jnp.where(lane < channels - rest, pltpu.roll(block, LANES - 2 * channels, 1), tail)
        conv_ref[3 * a + 2] = block[:, :channels]


def smem():
    return pl.BlockSpec(memory_space=pltpu.SMEM)


def kernel(body, name, operands, outs, flops, scratch=(), mib=16):
    specs = [smem() if value.ndim == 1 else pl.BlockSpec(value.shape, lambda n=value.ndim: (0,) * n) for value in operands]
    moved = sum(math.prod(value.shape) * value.dtype.itemsize for value in (*operands, *outs))
    return pl.pallas_call(
        body,
        in_specs=specs,
        out_specs=[pl.BlockSpec(out.shape, lambda n=out.ndim: (0,) * n) for out in outs],
        out_shape=outs,
        scratch_shapes=scratch,
        compiler_params=pltpu.CompilerParams(vmem_limit_bytes=mib * 1024 * 1024),
        cost_estimate=pl.CostEstimate(flops=flops, bytes_accessed=moved, transcendentals=0),
        name=name,
    )(*operands)


def exchange(chip_end, reverse, beside):
    came = [
        lax.ppermute(chip_end, "tm", x_shift(-step if reverse else step)) for step in range(1, XS)
    ]
    return lax.optimization_barrier((tuple(came), beside(chip_end)))


def own_frames(mine, got):
    early = place()[1] == 0
    return jnp.concatenate([jnp.where(early, mine, got), jnp.where(early, got, mine)], 0)


def all_sum(pack, recon):
    core = place()[1]
    second = core == 1
    mine = jnp.where(second, pack[1], pack[0])
    other = jnp.where(second, pack[0], pack[1])
    total = mine + lax.ppermute(other, "tm", CORE_SWAP)
    total, recon = lax.optimization_barrier((total, recon))
    frames = recon.shape[0] // CORES
    kept = jnp.where(second, recon[frames:], recon[:frames])
    got = lax.ppermute(jnp.where(second, recon[:frames], recon[frames:]), "tm", CORE_SWAP)
    beside = [
        (kept, got),
        lambda kept, got: jnp.stack(
            [jnp.where(second, got, kept), jnp.where(second, kept, got)], 0
        ).reshape(2, frames, recon.shape[1], -1, LANES),
    ]
    for axis, shift in (("tm", x_shift), ("rows", y_shift)):
        sent = total.astype(BF16)
        came = [lax.ppermute(sent, axis, shift(step)) for step in (1, 2, 3)]
        done = beside[0] if axis == "tm" else beside[1](*beside[0])
        came, done = lax.optimization_barrier((came, done))
        beside[0] = done
        came = [part.astype(F32) for part in came]
        total = (sent.astype(F32) + came[1]) + (came[0] + came[2])
    sent = jnp.broadcast_to(total.astype(BF16)[None], (ZS,) + total.shape)
    came = lax.all_to_all(sent, "rows", 0, 0, axis_index_groups=Z_GROUPS)
    mine = jnp.sum(came.astype(F32), axis=0)
    return mine, lax.ppermute(mine, "tm", CORE_SWAP), beside[0]


def shards(
    features, out_grad, decay_rate, clip_start, conv_kernel, context_mix, feature_mix, output_mix
):
    seqs, frames, channels, rows, cols = features.shape
    rows_count = lax.axis_size("rows")
    all_frames = frames * lax.axis_size("tm")
    height = rows * rows_count
    pixels = rows * cols
    count = CORES * frames
    scale_all = 1.0 / math.sqrt(seqs * all_frames * height * cols)
    scale_pix = 1.0 / math.sqrt(height * cols)
    chip, core = place()

    second = core == 1

    def share(array):
        mine = jnp.where(second, array[1], array[0])
        return mine, lax.ppermute(jnp.where(second, array[0], array[1]), "tm", CORE_SWAP)

    edge = jax.ShapeDtypeStruct((seqs, frames, channels, cols), BF16)
    to_inner, to_outer, to_core = kernel(
        cut_body,
        "cut",
        (features,),
        [edge, edge, jax.ShapeDtypeStruct(features.shape[1:], BF16)],
        1_000_000,
    )
    inner = lax.ppermute(to_inner, "rows", row_swap(0))
    outer = lax.ppermute(to_outer, "rows", row_swap(1))
    weights = jnp.concatenate([context_mix, feature_mix, output_mix.T], 0)
    x = own_frames(jnp.where(second, features[1], features[0]), lax.ppermute(to_core, "tm", CORE_SWAP))
    x = x.reshape(count, channels, pixels)
    (inner, outer), (x, weights) = lax.optimization_barrier(((inner, outer), (x, weights)))
    halo = jnp.stack([inner, outer], 0)
    got = lax.ppermute(jnp.where(second, halo[:, 0], halo[:, 1]), "tm", CORE_SWAP)

    taps_w = conv_kernel.reshape(3, 3, channels, channels).transpose(1, 3, 0, 2)
    taps_w = taps_w.reshape(3 * channels, 3 * channels)
    sds = jax.ShapeDtypeStruct
    full = (count, channels, pixels)
    state = sds((channels, pixels), BF16)

    update, chip_end, table, keep = kernel(
        conv_body,
        "conv",
        (clip_start, x, halo, got, taps_w, decay_rate),
        [
            sds(full, BF16),
            state,
            sds((count + 2 * (XS - 1), channels, LANES), F32),
            sds((count, 8, LANES), F32),
        ],
        340_000_000,
    )

    def cotangent(chip_end):
        late, _ = lax.optimization_barrier((out_grad, chip_end))
        return own_frames(*share(late)).reshape(count, channels, pixels)

    came, og = exchange(chip_end, False, cotangent)
    operands = (update, x, og, *came, table, keep, weights)
    (chip_end,) = kernel(
        join_body, "join", operands, [state], 200_000_000, [pltpu.VMEM(full, BF16)]
    )

    def mix_grad(chip_end):
        late, _ = lax.optimization_barrier((table, chip_end))
        return kernel(
            mix_grad_body,
            "mix_grad",
            (*operands[:6], late, *operands[7:]),
            [sds(full, F32), sds(full, F32), sds(full, BF16), sds((3 * channels, LANES), F32)],
            600_000_000,
        )

    came, (priors, prior_grads, recon, mixg) = exchange(chip_end, True, mix_grad)
    (pack,) = kernel(
        grad_body,
        "grad",
        (x, halo, got, priors, prior_grads, *came, table, keep, mixg),
        [sds((2, 3 * channels, LANES), F32)],
        340_000_000,
    )
    mine, got, recon = all_sum(pack, recon)
    taps_grad, ctx_grad, feat_grad, out_grad_t, decay_grad = kernel(
        functools.partial(unpack_body, scale_all=scale_all, scale_pix=scale_pix),
        "unpack",
        (mine, got),
        [
            sds((9, channels, channels), F32),
            sds(context_mix.shape, F32), sds(context_mix.shape, F32), sds(context_mix.shape, F32),
            sds((seqs, frames, channels), F32),
        ],
        1_000_000,
        mib=8,
    )
    return recon, decay_grad, taps_grad, ctx_grad, feat_grad, out_grad_t.T


def solution(mesh):
    split = P(None, "tm", None, "rows", None)
    in_specs = (split, split, P(), P(), P(), P(), P(), P())
    out_specs = (split, P(None, "tm", None), P(), P(), P(), P())
    return jax.shard_map(shards, mesh=mesh, in_specs=in_specs, out_specs=out_specs, check_vma=False)
```

```python
import functools
import math

import jax
import jax.numpy as jnp
from jax import lax
from jax.experimental import pallas as pl
from jax.experimental.pallas import tpu as pltpu
from jax.sharding import PartitionSpec as P

F32 = jnp.float32
BF16 = jnp.bfloat16
LANES = 128
CORES, XS, YS, ZS = 2, 4, 4, 8

CORE_SWAP = [(i, i ^ 1) for i in range(CORES * XS)]


def row_swap(first):
    pairs = [(i, i + 1) for i in range(first, YS * ZS - 1, 2)]
    return pairs + [(j, i) for i, j in pairs]


def x_shift(step):
    count = CORES * XS
    return [(i, (i + CORES * step) % count) for i in range(count)]


def y_shift(step):
    return [(i, i // YS * YS + (i + step) % YS) for i in range(YS * ZS)]


STEPS = (2, 1, 3)

Z_GROUPS = [[z * YS + y for z in range(ZS)] for y in range(YS)]


def mm(a, b):
    return jnp.dot(a, b, preferred_element_type=F32)


def mm_nt(a, b):
    return lax.dot_general(a, b, (((1,), (1,)), ((), ())), preferred_element_type=F32)


def shifted(value, step):
    lane = lax.broadcasted_iota(jnp.int32, (value.shape[0], LANES), 1)
    inside = lane < LANES - 1 if step > 0 else lane > 0
    blocks = []
    for at in range(0, value.shape[1], LANES):
        rolled = pltpu.roll(value[:, at : at + LANES], (-step) % LANES, 1)
        blocks.append(jnp.where(inside, rolled, 0.0))
    return jnp.concatenate(blocks, 1)


def wide(value, width):
    return jnp.concatenate([value] * (width // LANES), 1)


def row_taps(low, x, high):
    padded = jnp.concatenate([low, x, high], 1)
    width = x.shape[1]
    return jnp.concatenate([padded[:, LANES * a : LANES * a + width] for a in range(3)], 0)


def place():
    tm = lax.axis_index("tm")
    return tm // CORES, lax.rem(tm, CORES)


def halos(halo_ref, got_ref, f, frames):
    _, core = place()
    odd = lax.rem(lax.axis_index("rows"), 2)
    own = halo_ref.shape[2]
    at = f % own
    mine_first = core == 0 if f < own else core == 1
    return [
        jnp.where(mine_first, halo_ref[side, core, at], got_ref[side, at]) for side in (1 - odd, odd)
    ]


def cut_body(features_ref, inner_ref, outer_ref, share_ref):
    _, core = place()
    even = lax.rem(lax.axis_index("rows"), 2) == 0
    seqs, frames, _, rows, _ = features_ref.shape
    for s in range(seqs):
        for f in range(frames):
            value = features_ref[s, f].astype(F32)
            first, last = value[:, 0].astype(BF16), value[:, rows - 1].astype(BF16)
            inner_ref[s, f] = jnp.where(even, last, first)
            outer_ref[s, f] = jnp.where(even, first, last)
    for f in range(frames):
        share_ref[f] = features_ref[1 - core, f]


def conv_body(
    clip_ref, x_ref, halo_ref, got_ref, w_ref, decay_ref, upd_ref, end_ref, table_ref, keep_ref
):
    frames, channels, width = x_ref.shape
    chip, core = place()
    rates = decay_ref[core, pl.ds(pl.multiple_of(chip * frames, frames), frames)].T
    middle = []
    for at in range(1, XS - 1):
        product = None
        for f in range(at * frames, (at + 1) * frames):
            kept = jnp.where(clip_ref[core] == f, 0.0, 1.0) * decay_ref[core, f : f + 1]
            product = kept if product is None else product * kept
        middle.append(jnp.broadcast_to(product.T, (channels, LANES)))
    ones = jnp.ones((channels, LANES), F32)
    nought = jnp.zeros((channels, LANES), F32)
    both = middle[0] * middle[1]
    for at, weight in enumerate(
        [
            jnp.where(chip == 2, middle[0], jnp.where(chip == 3, middle[1], nought)),
            jnp.where(chip >= 1, ones, nought),
            jnp.where(chip == 3, both, nought),
            jnp.where(chip == 0, middle[0], jnp.where(chip == 1, middle[1], nought)),
            jnp.where(chip <= 2, ones, nought),
            jnp.where(chip == 0, both, nought),
        ]
    ):
        table_ref[frames + at] = weight
    state = jnp.zeros((channels, width), F32)
    for f in range(frames):
        gamma = jnp.broadcast_to(rates[:, f : f + 1], (channels, LANES))
        table_ref[f] = gamma
        keep = jnp.where(clip_ref[core] == chip * frames + f, 0.0, 1.0).astype(F32)
        keep_ref[f] = jnp.broadcast_to(keep, keep_ref.shape[1:])
        low, high = halos(halo_ref, got_ref, f, frames)
        y = mm(w_ref[...], row_taps(low, x_ref[f], high))
        out = (
            y[channels : 2 * channels]
            + shifted(y[:channels], -1)
            + shifted(y[2 * channels :], 1)
        ).astype(BF16)
        upd_ref[f] = out
        state = wide(gamma * keep, width) * state + out.astype(F32)
    end_ref[...] = state.astype(BF16)


def kept(keep_ref, f, value):
    rows, width = value.shape
    tile = jnp.concatenate([keep_ref[f]] * (rows // keep_ref.shape[1]), 0)
    return value * wide(tile, width)


GROUP = 4


def blocks(weight):
    blank = jnp.zeros_like(weight)
    return jnp.concatenate(
        [
            jnp.concatenate([weight if i == j else blank for j in range(GROUP)], 1)
            for i in range(GROUP)
        ],
        0,
    )


def join_weights(weights_ref):
    channels = weights_ref.shape[0] // 3
    turned = weights_ref[...].astype(F32).T
    row = lax.broadcasted_iota(jnp.int32, turned.shape, 1) < 2 * channels
    mix = jnp.concatenate([jnp.where(row, turned, 0.0), jnp.where(row, 0.0, turned)], 0)
    return mix.astype(BF16), blocks(weights_ref[:channels]), blocks(weights_ref[2 * channels :])


def entering(came_refs, table_ref, first):
    state = None
    for at, ref in enumerate(came_refs):
        term = wide(table_ref[first + at], ref.shape[1]) * ref[...].astype(F32)
        state = term if state is None else state + term
    return state


def prior_states(keep_ref, upd_ref, came_refs, table_ref):
    frames, _, width = upd_ref.shape
    state = entering(came_refs, table_ref, frames)
    for f in range(frames):
        prior = kept(keep_ref, f, state)
        yield prior
        if f + 1 < frames:
            state = wide(table_ref[f], width) * prior + upd_ref[f].astype(F32)


def gates(preact, hidden_grad):
    gate = 0.5 * jnp.tanh(0.5 * preact) + 0.5
    pre_grad = (hidden_grad * gate * (1.0 + preact * (1.0 - gate))).astype(BF16)
    return gate, pre_grad


def join_body(
    upd_ref, x_ref, og_ref, came1_ref, came2_ref, came3_ref, table_ref, keep_ref, weights_ref,
    end_ref, low_ref,
):
    frames, channels, width = x_ref.shape
    hidden_count = weights_ref.shape[1]
    mix, ctx, _ = join_weights(weights_ref)
    came = (came1_ref, came2_ref, came3_ref)
    for f, prior in enumerate(prior_states(keep_ref, upd_ref, came, table_ref)):
        low_ref[f] = prior.astype(BF16)
    back = jnp.zeros((channels, width), F32)
    for f in reversed(range(0, frames, GROUP)):
        pre_grads = []
        for i in range(f, f + GROUP):
            both = mm(mix, jnp.concatenate([low_ref[i], x_ref[i], og_ref[i]], 0))
            pre_grads.append(gates(both[:hidden_count], both[hidden_count:])[1])
        prior_grad = mm(ctx, jnp.concatenate(pre_grads, 0))
        for i in reversed(range(GROUP)):
            grad = prior_grad[i * channels : (i + 1) * channels]
            back = kept(keep_ref, f + i, wide(table_ref[f + i], width) * back + grad)
    end_ref[...] = back.astype(BF16)


def mix_grad_body(
    upd_ref, x_ref, og_ref, came1_ref, came2_ref, came3_ref, table_ref, keep_ref, weights_ref,
    prior_ref, pgrad_ref, recon_ref, mixg_ref,
):
    channels = x_ref.shape[1]
    hidden_count = weights_ref.shape[1]
    mix, ctx, out_t = join_weights(weights_ref)
    came = (came1_ref, came2_ref, came3_ref)
    total = jnp.zeros(mixg_ref.shape, F32)
    hiddens, pre_grads = [], []
    for f, prior in enumerate(prior_states(keep_ref, upd_ref, came, table_ref)):
        prior_ref[f] = prior
        joined = jnp.concatenate([prior.astype(BF16), x_ref[f], og_ref[f]], 0)
        both = mm(mix, joined)
        preact = both[:hidden_count]
        gate, pre_grad = gates(preact, both[hidden_count:])
        hiddens.append((preact * gate).astype(BF16))
        pre_grads.append(pre_grad)
        total = total + mm_nt(joined, jnp.concatenate([pre_grad, hiddens[-1]], 0))
        if len(hiddens) < GROUP:
            continue
        prior_grad = mm(ctx, jnp.concatenate(pre_grads, 0))
        recon = mm(out_t, jnp.concatenate(hiddens, 0)).astype(BF16)
        for i in range(GROUP):
            pgrad_ref[f + 1 - GROUP + i] = prior_grad[i * channels : (i + 1) * channels]
            recon_ref[f + 1 - GROUP + i] = recon[i * channels : (i + 1) * channels]
        hiddens, pre_grads = [], []
    mixg_ref[...] = total


def grad_body(
    x_ref, halo_ref, got_ref, prior_ref, pgrad_ref, came1_ref, came2_ref, came3_ref, table_ref,
    keep_ref, mixg_ref, pack_ref,
):
    frames, channels, width = x_ref.shape
    taps_rows = 3 * channels
    half = LANES // 2
    rest = taps_rows - LANES
    chip, core = place()
    lane = lax.broadcasted_iota(jnp.int32, (channels, LANES), 1)
    state = entering((came1_ref, came2_ref, came3_ref), table_ref, frames + XS - 1)
    total = jnp.zeros((taps_rows, taps_rows), F32)
    decay_grad = jnp.zeros((channels, LANES), F32)
    for f in reversed(range(frames)):
        product = prior_ref[f] * state
        folded = product[:, :LANES]
        for at in range(LANES, width, LANES):
            folded = folded + product[:, at : at + LANES]
        column = jnp.sum(folded, axis=1, keepdims=True)
        slot = (chip * CORES + core) * frames + f
        decay_grad = decay_grad + jnp.where(lane == slot, column, 0.0)
        u = jnp.concatenate(
            [shifted(state, 1).astype(BF16), state.astype(BF16), shifted(state, -1).astype(BF16)], 0
        )
        low, high = halos(halo_ref, got_ref, f, frames)
        taps = row_taps(low, x_ref[f], high)
        total = total + mm_nt(taps, u)
        if f:
            state = kept(keep_ref, f, wide(table_ref[f], width) * state + pgrad_ref[f])
    pack_ref[0] = total[:, :LANES]
    second = jnp.concatenate([total[:, LANES:], jnp.zeros((taps_rows, LANES - rest), F32)], 1)
    second = pltpu.roll(second, half, 1)
    wide_lane = lax.broadcasted_iota(jnp.int32, (2 * channels, LANES), 1)
    pack_ref[1, : 2 * channels] = second[: 2 * channels] + jnp.where(
        wide_lane < half, mixg_ref[: 2 * channels], 0.0
    )
    pack_ref[1, :channels] += pltpu.roll(second[2 * channels :], rest, 1)
    pack_ref[1, 2 * channels :] = decay_grad + jnp.where(lane >= half, mixg_ref[2 * channels :], 0.0)


def unpack_body(mine_ref, got_ref, conv_ref, ctx_ref, feat_ref, out_t_ref, decay_ref, *, scale_all, scale_pix):
    channels, half = ctx_ref.shape
    taps_rows = 3 * channels
    rest = taps_rows - LANES
    chip, core = place()
    mine = mine_ref[...]
    got = got_ref[...]
    first = jnp.where(core == 0, mine, got)
    second = jnp.where(core == 0, got, mine)
    ctx_ref[...] = second[:channels, :half] * scale_all
    feat_ref[...] = second[channels : 2 * channels, :half] * scale_all
    last = second[2 * channels : taps_rows]
    out_t_ref[...] = pltpu.roll(last, half, 1)[:, :half] * scale_all
    seqs, frames, _ = decay_ref.shape
    first_lane = (chip * seqs * CORES + core) * frames
    slots = pltpu.roll(last, LANES - first_lane, 1).T * scale_pix
    for s in range(seqs):
        decay_ref[s] = slots[s * CORES * frames : s * CORES * frames + frames]
    lane = lax.broadcasted_iota(jnp.int32, (channels, LANES), 1)
    for a in range(3):
        block = first[a * channels : (a + 1) * channels] * scale_all
        tail = second[:channels] if a == 2 else second[a * channels : (a + 1) * channels]
        at = half + (rest if a == 2 else 0)
        tail = pltpu.roll(tail * scale_all, (channels - rest - at) % LANES, 1)
        conv_ref[3 * a] = block[:, :channels]
        conv_ref[3 * a + 1] = pltpu.roll(block, LANES - channels, 1)[:, :channels]
        block = jnp.where(lane < channels - rest, pltpu.roll(block, LANES - 2 * channels, 1), tail)
        conv_ref[3 * a + 2] = block[:, :channels]


def smem():
    return pl.BlockSpec(memory_space=pltpu.SMEM)


def kernel(body, name, operands, outs, flops, scratch=(), mib=16):
    specs = [smem() if value.ndim == 1 else pl.BlockSpec(value.shape, lambda n=value.ndim: (0,) * n) for value in operands]
    moved = sum(math.prod(value.shape) * value.dtype.itemsize for value in (*operands, *outs))
    return pl.pallas_call(
        body,
        in_specs=specs,
        out_specs=[pl.BlockSpec(out.shape, lambda n=out.ndim: (0,) * n) for out in outs],
        out_shape=outs,
        scratch_shapes=scratch,
        compiler_params=pltpu.CompilerParams(vmem_limit_bytes=mib * 1024 * 1024),
        cost_estimate=pl.CostEstimate(flops=flops, bytes_accessed=moved, transcendentals=0),
        name=name,
    )(*operands)


def exchange(chip_end, reverse, beside):
    came = [
        lax.ppermute(chip_end, "tm", x_shift(-step if reverse else step)) for step in STEPS
    ]
    return lax.optimization_barrier((tuple(came), beside(chip_end)))


def own_frames(mine, got):
    early = place()[1] == 0
    return jnp.concatenate([jnp.where(early, mine, got), jnp.where(early, got, mine)], 0)


def all_sum(pack, recon):
    core = place()[1]
    second = core == 1
    mine = jnp.where(second, pack[1], pack[0])
    other = jnp.where(second, pack[0], pack[1])
    total = mine + lax.ppermute(other, "tm", CORE_SWAP)
    total, recon = lax.optimization_barrier((total, recon))
    frames = recon.shape[0] // CORES
    kept = jnp.where(second, recon[frames:], recon[:frames])
    got = lax.ppermute(jnp.where(second, recon[:frames], recon[frames:]), "tm", CORE_SWAP)
    beside = [
        (kept, got),
        lambda kept, got: jnp.stack(
            [jnp.where(second, got, kept), jnp.where(second, kept, got)], 0
        ).reshape(2, frames, recon.shape[1], -1, LANES),
    ]
    for axis, shift in (("tm", x_shift), ("rows", y_shift)):
        sent = total.astype(BF16)
        came = [lax.ppermute(sent, axis, shift(step)) for step in STEPS]
        done = beside[0] if axis == "tm" else beside[1](*beside[0])
        came, done = lax.optimization_barrier((came, done))
        beside[0] = done
        came = [part.astype(F32) for part in came]
        total = (came[0] + sent.astype(F32)) + (came[1] + came[2])
    sent = jnp.broadcast_to(total.astype(BF16)[None], (ZS,) + total.shape)
    came = lax.all_to_all(sent, "rows", 0, 0, axis_index_groups=Z_GROUPS)
    mine = jnp.sum(came.astype(F32), axis=0)
    return mine, lax.ppermute(mine, "tm", CORE_SWAP), beside[0]


def shards(
    features, out_grad, decay_rate, clip_start, conv_kernel, context_mix, feature_mix, output_mix
):
    seqs, frames, channels, rows, cols = features.shape
    rows_count = lax.axis_size("rows")
    all_frames = frames * lax.axis_size("tm")
    height = rows * rows_count
    pixels = rows * cols
    count = CORES * frames
    scale_all = 1.0 / math.sqrt(seqs * all_frames * height * cols)
    scale_pix = 1.0 / math.sqrt(height * cols)
    chip, core = place()

    second = core == 1

    def share(array):
        mine = jnp.where(second, array[1], array[0])
        return mine, lax.ppermute(jnp.where(second, array[0], array[1]), "tm", CORE_SWAP)

    edge = jax.ShapeDtypeStruct((seqs, frames, channels, cols), BF16)
    to_inner, to_outer, to_core = kernel(
        cut_body,
        "cut",
        (features,),
        [edge, edge, jax.ShapeDtypeStruct(features.shape[1:], BF16)],
        1_000_000,
    )
    inner = lax.ppermute(to_inner, "rows", row_swap(0))
    outer = lax.ppermute(to_outer, "rows", row_swap(1))
    weights = jnp.concatenate([context_mix, feature_mix, output_mix.T], 0)
    x = own_frames(jnp.where(second, features[1], features[0]), lax.ppermute(to_core, "tm", CORE_SWAP))
    x = x.reshape(count, channels, pixels)
    (inner, outer), (x, weights) = lax.optimization_barrier(((inner, outer), (x, weights)))
    halo = jnp.stack([inner, outer], 0)
    got = lax.ppermute(jnp.where(second, halo[:, 0], halo[:, 1]), "tm", CORE_SWAP)

    taps_w = conv_kernel.reshape(3, 3, channels, channels).transpose(1, 3, 0, 2)
    taps_w = taps_w.reshape(3 * channels, 3 * channels)
    sds = jax.ShapeDtypeStruct
    full = (count, channels, pixels)
    state = sds((channels, pixels), BF16)

    update, chip_end, table, keep = kernel(
        conv_body,
        "conv",
        (clip_start, x, halo, got, taps_w, decay_rate),
        [
            sds(full, BF16),
            state,
            sds((count + 2 * (XS - 1), channels, LANES), F32),
            sds((count, 8, LANES), F32),
        ],
        340_000_000,
    )

    def cotangent(chip_end):
        late, _ = lax.optimization_barrier((out_grad, chip_end))
        return own_frames(*share(late)).reshape(count, channels, pixels)

    came, og = exchange(chip_end, False, cotangent)
    operands = (update, x, og, *came, table, keep, weights)
    (chip_end,) = kernel(
        join_body, "join", operands, [state], 200_000_000, [pltpu.VMEM(full, BF16)]
    )

    def mix_grad(chip_end):
        late, _ = lax.optimization_barrier((table, chip_end))
        return kernel(
            mix_grad_body,
            "mix_grad",
            (*operands[:6], late, *operands[7:]),
            [sds(full, F32), sds(full, F32), sds(full, BF16), sds((3 * channels, LANES), F32)],
            600_000_000,
        )

    came, (priors, prior_grads, recon, mixg) = exchange(chip_end, True, mix_grad)
    (pack,) = kernel(
        grad_body,
        "grad",
        (x, halo, got, priors, prior_grads, *came, table, keep, mixg),
        [sds((2, 3 * channels, LANES), F32)],
        340_000_000,
    )
    mine, got, recon = all_sum(pack, recon)
    taps_grad, ctx_grad, feat_grad, out_grad_t, decay_grad = kernel(
        functools.partial(unpack_body, scale_all=scale_all, scale_pix=scale_pix),
        "unpack",
        (mine, got),
        [
            sds((9, channels, channels), F32),
            sds(context_mix.shape, F32), sds(context_mix.shape, F32), sds(context_mix.shape, F32),
            sds((seqs, frames, channels), F32),
        ],
        1_000_000,
        mib=8,
    )
    return recon, decay_grad, taps_grad, ctx_grad, feat_grad, out_grad_t.T


def solution(mesh):
    split = P(None, "tm", None, "rows", None)
    in_specs = (split, split, P(), P(), P(), P(), P(), P())
    out_specs = (split, P(None, "tm", None), P(), P(), P(), P())
    return jax.shard_map(shards, mesh=mesh, in_specs=in_specs, out_specs=out_specs, check_vma=False)
```

```python
import functools
import math

import jax
import jax.numpy as jnp
from jax import lax
from jax.experimental import pallas as pl
from jax.experimental.pallas import tpu as pltpu
from jax.sharding import PartitionSpec as P

F32 = jnp.float32
BF16 = jnp.bfloat16
LANES = 128
CORES, XS, YS, ZS = 2, 4, 4, 8

CORE_SWAP = [(i, i ^ 1) for i in range(CORES * XS)]


def row_swap(first):
    pairs = [(i, i + 1) for i in range(first, YS * ZS - 1, 2)]
    return pairs + [(j, i) for i, j in pairs]


def x_shift(step):
    count = CORES * XS
    return [(i, (i + CORES * step) % count) for i in range(count)]


def y_shift(step):
    return [(i, i // YS * YS + (i + step) % YS) for i in range(YS * ZS)]


STEPS = (2, 1, 3)

Z_GROUPS = [[z * YS + y for z in range(ZS)] for y in range(YS)]


def mm(a, b):
    return jnp.dot(a, b, preferred_element_type=F32)


def mm_nt(a, b):
    return lax.dot_general(a, b, (((1,), (1,)), ((), ())), preferred_element_type=F32)


def shifted(value, step):
    lane = lax.broadcasted_iota(jnp.int32, (value.shape[0], LANES), 1)
    inside = lane < LANES - 1 if step > 0 else lane > 0
    blocks = []
    for at in range(0, value.shape[1], LANES):
        rolled = pltpu.roll(value[:, at : at + LANES], (-step) % LANES, 1)
        blocks.append(jnp.where(inside, rolled, 0.0))
    return jnp.concatenate(blocks, 1)


def wide(value, width):
    return jnp.concatenate([value] * (width // LANES), 1)


def row_taps(low, x, high):
    padded = jnp.concatenate([low, x, high], 1)
    width = x.shape[1]
    return jnp.concatenate([padded[:, LANES * a : LANES * a + width] for a in range(3)], 0)


def place():
    tm = lax.axis_index("tm")
    return tm // CORES, lax.rem(tm, CORES)


def halos(halo_ref, got_ref, f, frames):
    _, core = place()
    odd = lax.rem(lax.axis_index("rows"), 2)
    own = halo_ref.shape[2]
    at = f % own
    mine_first = core == 0 if f < own else core == 1
    return [
        jnp.where(mine_first, halo_ref[side, core, at], got_ref[side, at]) for side in (odd, 1 - odd)
    ]


def cut_body(features_ref, inner_ref, outer_ref, share_ref):
    _, core = place()
    even = lax.rem(lax.axis_index("rows"), 2) == 0
    seqs, frames, _, rows, _ = features_ref.shape
    for s in range(seqs):
        for f in range(frames):
            value = features_ref[s, f].astype(F32)
            first, last = value[:, 0].astype(BF16), value[:, rows - 1].astype(BF16)
            inner_ref[s, f] = jnp.where(even, last, first)
            outer_ref[s, f] = jnp.where(even, first, last)
    for f in range(frames):
        share_ref[f] = features_ref[1 - core, f]


def conv_body(
    clip_ref, x_ref, halo_ref, got_ref, w_ref, decay_ref, upd_ref, end_ref, table_ref, keep_ref
):
    frames, channels, width = x_ref.shape
    chip, core = place()
    rates = decay_ref[core, pl.ds(pl.multiple_of(chip * frames, frames), frames)].T
    middle = []
    for at in range(1, XS - 1):
        product = None
        for f in range(at * frames, (at + 1) * frames):
            kept = jnp.where(clip_ref[core] == f, 0.0, 1.0) * decay_ref[core, f : f + 1]
            product = kept if product is None else product * kept
        middle.append(jnp.broadcast_to(product.T, (channels, LANES)))
    ones = jnp.ones((channels, LANES), F32)
    nought = jnp.zeros((channels, LANES), F32)
    both = middle[0] * middle[1]
    for at, weight in enumerate(
        [
            jnp.where(chip == 2, middle[0], jnp.where(chip == 3, middle[1], nought)),
            jnp.where(chip >= 1, ones, nought),
            jnp.where(chip == 3, both, nought),
            jnp.where(chip == 0, middle[0], jnp.where(chip == 1, middle[1], nought)),
            jnp.where(chip <= 2, ones, nought),
            jnp.where(chip == 0, both, nought),
        ]
    ):
        table_ref[frames + at] = weight
    state = jnp.zeros((channels, width), F32)
    for f in range(frames):
        gamma = jnp.broadcast_to(rates[:, f : f + 1], (channels, LANES))
        table_ref[f] = gamma
        keep = jnp.where(clip_ref[core] == chip * frames + f, 0.0, 1.0).astype(F32)
        keep_ref[f] = jnp.broadcast_to(keep, keep_ref.shape[1:])
        low, high = halos(halo_ref, got_ref, f, frames)
        y = mm(w_ref[...], row_taps(low, x_ref[f], high))
        out = (
            y[channels : 2 * channels]
            + shifted(y[:channels], -1)
            + shifted(y[2 * channels :], 1)
        ).astype(BF16)
        upd_ref[f] = out
        state = wide(gamma * keep, width) * state + out.astype(F32)
    end_ref[...] = state.astype(BF16)


def kept(keep_ref, f, value):
    rows, width = value.shape
    tile = jnp.concatenate([keep_ref[f]] * (rows // keep_ref.shape[1]), 0)
    return value * wide(tile, width)


GROUP = 4


def blocks(weight):
    blank = jnp.zeros_like(weight)
    return jnp.concatenate(
        [
            jnp.concatenate([weight if i == j else blank for j in range(GROUP)], 1)
            for i in range(GROUP)
        ],
        0,
    )


def join_weights(weights_ref):
    channels = weights_ref.shape[0] // 3
    turned = weights_ref[...].astype(F32).T
    row = lax.broadcasted_iota(jnp.int32, turned.shape, 1) < 2 * channels
    mix = jnp.concatenate([jnp.where(row, turned, 0.0), jnp.where(row, 0.0, turned)], 0)
    return mix.astype(BF16), blocks(weights_ref[:channels]), blocks(weights_ref[2 * channels :])


def entering(came_refs, table_ref, first):
    state = None
    for at, ref in enumerate(came_refs):
        term = wide(table_ref[first + at], ref.shape[1]) * ref[...].astype(F32)
        state = term if state is None else state + term
    return state


def prior_states(keep_ref, upd_ref, came_refs, table_ref):
    frames, _, width = upd_ref.shape
    state = entering(came_refs, table_ref, frames)
    for f in range(frames):
        prior = kept(keep_ref, f, state)
        yield prior
        if f + 1 < frames:
            state = wide(table_ref[f], width) * prior + upd_ref[f].astype(F32)


def gates(preact, hidden_grad):
    gate = 0.5 * jnp.tanh(0.5 * preact) + 0.5
    pre_grad = (hidden_grad * gate * (1.0 + preact * (1.0 - gate))).astype(BF16)
    return gate, pre_grad


def join_body(
    upd_ref, x_ref, og_ref, came1_ref, came2_ref, came3_ref, table_ref, keep_ref, weights_ref,
    end_ref, low_ref,
):
    frames, channels, width = x_ref.shape
    hidden_count = weights_ref.shape[1]
    mix, ctx, _ = join_weights(weights_ref)
    came = (came1_ref, came2_ref, came3_ref)
    for f, prior in enumerate(prior_states(keep_ref, upd_ref, came, table_ref)):
        low_ref[f] = prior.astype(BF16)
    back = jnp.zeros((channels, width), F32)
    for f in reversed(range(0, frames, GROUP)):
        pre_grads = []
        for i in range(f, f + GROUP):
            both = mm(mix, jnp.concatenate([low_ref[i], x_ref[i], og_ref[i]], 0))
            pre_grads.append(gates(both[:hidden_count], both[hidden_count:])[1])
        prior_grad = mm(ctx, jnp.concatenate(pre_grads, 0))
        for i in reversed(range(GROUP)):
            grad = prior_grad[i * channels : (i + 1) * channels]
            back = kept(keep_ref, f + i, wide(table_ref[f + i], width) * back + grad)
    end_ref[...] = back.astype(BF16)


def mix_grad_body(
    upd_ref, x_ref, og_ref, came1_ref, came2_ref, came3_ref, table_ref, keep_ref, weights_ref,
    prior_ref, pgrad_ref, recon_ref, mixg_ref,
):
    channels = x_ref.shape[1]
    hidden_count = weights_ref.shape[1]
    mix, ctx, out_t = join_weights(weights_ref)
    came = (came1_ref, came2_ref, came3_ref)
    total = jnp.zeros(mixg_ref.shape, F32)
    hiddens, pre_grads = [], []
    for f, prior in enumerate(prior_states(keep_ref, upd_ref, came, table_ref)):
        prior_ref[f] = prior
        joined = jnp.concatenate([prior.astype(BF16), x_ref[f], og_ref[f]], 0)
        both = mm(mix, joined)
        preact = both[:hidden_count]
        gate, pre_grad = gates(preact, both[hidden_count:])
        hiddens.append((preact * gate).astype(BF16))
        pre_grads.append(pre_grad)
        total = total + mm_nt(joined, jnp.concatenate([pre_grad, hiddens[-1]], 0))
        if len(hiddens) < GROUP:
            continue
        prior_grad = mm(ctx, jnp.concatenate(pre_grads, 0))
        recon = mm(out_t, jnp.concatenate(hiddens, 0)).astype(BF16)
        for i in range(GROUP):
            pgrad_ref[f + 1 - GROUP + i] = prior_grad[i * channels : (i + 1) * channels]
            recon_ref[f + 1 - GROUP + i] = recon[i * channels : (i + 1) * channels]
        hiddens, pre_grads = [], []
    mixg_ref[...] = total


def grad_body(
    x_ref, halo_ref, got_ref, prior_ref, pgrad_ref, came1_ref, came2_ref, came3_ref, table_ref,
    keep_ref, mixg_ref, pack_ref,
):
    frames, channels, width = x_ref.shape
    taps_rows = 3 * channels
    half = LANES // 2
    rest = taps_rows - LANES
    chip, core = place()
    lane = lax.broadcasted_iota(jnp.int32, (channels, LANES), 1)
    state = entering((came1_ref, came2_ref, came3_ref), table_ref, frames + XS - 1)
    total = jnp.zeros((taps_rows, taps_rows), F32)
    decay_grad = jnp.zeros((channels, LANES), F32)
    for f in reversed(range(frames)):
        product = prior_ref[f] * state
        folded = product[:, :LANES]
        for at in range(LANES, width, LANES):
            folded = folded + product[:, at : at + LANES]
        column = jnp.sum(folded, axis=1, keepdims=True)
        slot = (chip * CORES + core) * frames + f
        decay_grad = decay_grad + jnp.where(lane == slot, column, 0.0)
        u = jnp.concatenate(
            [shifted(state, 1).astype(BF16), state.astype(BF16), shifted(state, -1).astype(BF16)], 0
        )
        low, high = halos(halo_ref, got_ref, f, frames)
        taps = row_taps(low, x_ref[f], high)
        total = total + mm_nt(taps, u)
        if f:
            state = kept(keep_ref, f, wide(table_ref[f], width) * state + pgrad_ref[f])
    pack_ref[0] = total[:, :LANES]
    second = jnp.concatenate([total[:, LANES:], jnp.zeros((taps_rows, LANES - rest), F32)], 1)
    second = pltpu.roll(second, half, 1)
    wide_lane = lax.broadcasted_iota(jnp.int32, (2 * channels, LANES), 1)
    pack_ref[1, : 2 * channels] = second[: 2 * channels] + jnp.where(
        wide_lane < half, mixg_ref[: 2 * channels], 0.0
    )
    pack_ref[1, :channels] += pltpu.roll(second[2 * channels :], rest, 1)
    pack_ref[1, 2 * channels :] = decay_grad + jnp.where(lane >= half, mixg_ref[2 * channels :], 0.0)


def unpack_body(mine_ref, got_ref, conv_ref, ctx_ref, feat_ref, out_t_ref, decay_ref, *, scale_all, scale_pix):
    channels, half = ctx_ref.shape
    taps_rows = 3 * channels
    rest = taps_rows - LANES
    chip, core = place()
    mine = mine_ref[...]
    got = got_ref[...]
    first = jnp.where(core == 0, mine, got)
    second = jnp.where(core == 0, got, mine)
    ctx_ref[...] = second[:channels, :half] * scale_all
    feat_ref[...] = second[channels : 2 * channels, :half] * scale_all
    last = second[2 * channels : taps_rows]
    out_t_ref[...] = pltpu.roll(last, half, 1)[:, :half] * scale_all
    seqs, frames, _ = decay_ref.shape
    first_lane = (chip * seqs * CORES + core) * frames
    slots = pltpu.roll(last, LANES - first_lane, 1).T * scale_pix
    for s in range(seqs):
        decay_ref[s] = slots[s * CORES * frames : s * CORES * frames + frames]
    lane = lax.broadcasted_iota(jnp.int32, (channels, LANES), 1)
    for a in range(3):
        block = first[a * channels : (a + 1) * channels] * scale_all
        tail = second[:channels] if a == 2 else second[a * channels : (a + 1) * channels]
        at = half + (rest if a == 2 else 0)
        tail = pltpu.roll(tail * scale_all, (channels - rest - at) % LANES, 1)
        conv_ref[3 * a] = block[:, :channels]
        conv_ref[3 * a + 1] = pltpu.roll(block, LANES - channels, 1)[:, :channels]
        block = jnp.where(lane < channels - rest, pltpu.roll(block, LANES - 2 * channels, 1), tail)
        conv_ref[3 * a + 2] = block[:, :channels]


def smem():
    return pl.BlockSpec(memory_space=pltpu.SMEM)


def kernel(body, name, operands, outs, flops, scratch=(), mib=16):
    specs = [smem() if value.ndim == 1 else pl.BlockSpec(value.shape, lambda n=value.ndim: (0,) * n) for value in operands]
    moved = sum(math.prod(value.shape) * value.dtype.itemsize for value in (*operands, *outs))
    return pl.pallas_call(
        body,
        in_specs=specs,
        out_specs=[pl.BlockSpec(out.shape, lambda n=out.ndim: (0,) * n) for out in outs],
        out_shape=outs,
        scratch_shapes=scratch,
        compiler_params=pltpu.CompilerParams(vmem_limit_bytes=mib * 1024 * 1024),
        cost_estimate=pl.CostEstimate(flops=flops, bytes_accessed=moved, transcendentals=0),
        name=name,
    )(*operands)


def exchange(chip_end, reverse, beside):
    came = [
        lax.ppermute(chip_end, "tm", x_shift(-step if reverse else step)) for step in STEPS
    ]
    return lax.optimization_barrier((tuple(came), beside(chip_end)))


def own_frames(mine, got):
    early = place()[1] == 0
    return jnp.concatenate([jnp.where(early, mine, got), jnp.where(early, got, mine)], 0)


def all_sum(pack, recon):
    core = place()[1]
    second = core == 1
    mine = jnp.where(second, pack[1], pack[0])
    other = jnp.where(second, pack[0], pack[1])
    total = mine + lax.ppermute(other, "tm", CORE_SWAP)
    total, recon = lax.optimization_barrier((total, recon))
    frames = recon.shape[0] // CORES
    kept = jnp.where(second, recon[frames:], recon[:frames])
    got = lax.ppermute(jnp.where(second, recon[:frames], recon[frames:]), "tm", CORE_SWAP)
    beside = [
        (kept, got),
        lambda kept, got: jnp.stack(
            [jnp.where(second, got, kept), jnp.where(second, kept, got)], 0
        ).reshape(2, frames, recon.shape[1], -1, LANES),
    ]
    for axis, shift in (("tm", x_shift), ("rows", y_shift)):
        sent = total.astype(BF16)
        came = [lax.ppermute(sent, axis, shift(step)) for step in STEPS]
        done = beside[0] if axis == "tm" else beside[1](*beside[0])
        came, done = lax.optimization_barrier((came, done))
        beside[0] = done
        came = [part.astype(F32) for part in came]
        total = (came[0] + sent.astype(F32)) + (came[1] + came[2])
    sent = jnp.broadcast_to(total.astype(BF16)[None], (ZS,) + total.shape)
    came = lax.all_to_all(sent, "rows", 0, 0, axis_index_groups=Z_GROUPS)
    mine = jnp.sum(came.astype(F32), axis=0)
    return mine, lax.ppermute(mine, "tm", CORE_SWAP), beside[0]


def shards(
    features, out_grad, decay_rate, clip_start, conv_kernel, context_mix, feature_mix, output_mix
):
    seqs, frames, channels, rows, cols = features.shape
    rows_count = lax.axis_size("rows")
    all_frames = frames * lax.axis_size("tm")
    height = rows * rows_count
    pixels = rows * cols
    count = CORES * frames
    scale_all = 1.0 / math.sqrt(seqs * all_frames * height * cols)
    scale_pix = 1.0 / math.sqrt(height * cols)
    chip, core = place()

    second = core == 1

    def share(array):
        mine = jnp.where(second, array[1], array[0])
        return mine, lax.ppermute(jnp.where(second, array[0], array[1]), "tm", CORE_SWAP)

    edge = jax.ShapeDtypeStruct((seqs, frames, channels, cols), BF16)
    to_inner, to_outer, to_core = kernel(
        cut_body,
        "cut",
        (features,),
        [edge, edge, jax.ShapeDtypeStruct(features.shape[1:], BF16)],
        1_000_000,
    )
    outer = lax.ppermute(to_outer, "rows", row_swap(1))
    inner = lax.ppermute(to_inner, "rows", row_swap(0))
    weights = jnp.concatenate([context_mix, feature_mix, output_mix.T], 0)
    x = own_frames(jnp.where(second, features[1], features[0]), lax.ppermute(to_core, "tm", CORE_SWAP))
    x = x.reshape(count, channels, pixels)
    (outer, inner), (x, weights) = lax.optimization_barrier(((outer, inner), (x, weights)))
    halo = jnp.stack([outer, inner], 0)
    got = lax.ppermute(jnp.where(second, halo[:, 0], halo[:, 1]), "tm", CORE_SWAP)

    taps_w = conv_kernel.reshape(3, 3, channels, channels).transpose(1, 3, 0, 2)
    taps_w = taps_w.reshape(3 * channels, 3 * channels)
    sds = jax.ShapeDtypeStruct
    full = (count, channels, pixels)
    state = sds((channels, pixels), BF16)

    update, chip_end, table, keep = kernel(
        conv_body,
        "conv",
        (clip_start, x, halo, got, taps_w, decay_rate),
        [
            sds(full, BF16),
            state,
            sds((count + 2 * (XS - 1), channels, LANES), F32),
            sds((count, 8, LANES), F32),
        ],
        340_000_000,
    )

    def cotangent(chip_end):
        late, _ = lax.optimization_barrier((out_grad, chip_end))
        return own_frames(*share(late)).reshape(count, channels, pixels)

    came, og = exchange(chip_end, False, cotangent)
    operands = (update, x, og, *came, table, keep, weights)
    (chip_end,) = kernel(
        join_body, "join", operands, [state], 200_000_000, [pltpu.VMEM(full, BF16)]
    )

    def mix_grad(chip_end):
        late, _ = lax.optimization_barrier((table, chip_end))
        return kernel(
            mix_grad_body,
            "mix_grad",
            (*operands[:6], late, *operands[7:]),
            [sds(full, F32), sds(full, F32), sds(full, BF16), sds((3 * channels, LANES), F32)],
            600_000_000,
        )

    came, (priors, prior_grads, recon, mixg) = exchange(chip_end, True, mix_grad)
    (pack,) = kernel(
        grad_body,
        "grad",
        (x, halo, got, priors, prior_grads, *came, table, keep, mixg),
        [sds((2, 3 * channels, LANES), F32)],
        340_000_000,
    )
    mine, got, recon = all_sum(pack, recon)
    taps_grad, ctx_grad, feat_grad, out_grad_t, decay_grad = kernel(
        functools.partial(unpack_body, scale_all=scale_all, scale_pix=scale_pix),
        "unpack",
        (mine, got),
        [
            sds((9, channels, channels), F32),
            sds(context_mix.shape, F32), sds(context_mix.shape, F32), sds(context_mix.shape, F32),
            sds((seqs, frames, channels), F32),
        ],
        1_000_000,
        mib=8,
    )
    return recon, decay_grad, taps_grad, ctx_grad, feat_grad, out_grad_t.T


def solution(mesh):
    split = P(None, "tm", None, "rows", None)
    in_specs = (split, split, P(), P(), P(), P(), P(), P())
    out_specs = (split, P(None, "tm", None), P(), P(), P(), P())
    return jax.shard_map(shards, mesh=mesh, in_specs=in_specs, out_specs=out_specs, check_vma=False)
```
